32 devices in a mesh: ctx: 8 (over y, x, core), hs: 4 (over z).
Axes of the slice: x: 2, y: 2, z: 4, core: 2. Of those that a mesh axis runs over, the one named last changes fastest.
Arguments:
- queries: bfloat16 [4096, 4096], P(('ctx', 'hs')), may hold values from -6 to 6
- key_matrix: bfloat16 [4096, 512], P(('ctx', 'hs')), may hold values from -6 to 6
- value_matrix: bfloat16 [4096, 512], P(('ctx', 'hs')), may hold values from -6 to 6
- output_gradient: bfloat16 [4096, 4096], P(('ctx', 'hs')), may hold values from -6 to 6
- doc_lengths: int32 [8], replicated, may hold values from 1 to 2048, 4096 in all
- windows: int32 [32], replicated, may hold values from 32 to 256, as said below
Outputs:
- query_grad: bfloat16 [4096, 4096], P(('ctx', 'hs'))
- key_grad: bfloat16 [4096, 512], P(('ctx', 'hs'))
The draws below stay inside these ranges and needn't reach their ends.
Inputs may be any that keep to these rules, and one draw needn't show every extreme that they name: `doc_lengths`: the document lengths sum to 4096; the longest is exactly 2048. `windows`: A head's window counts the positions it may see, its own included; some head's window is exactly 256.
All inputs are finite; a program needn't handle non-finite values.
Results may differ from the reference program's by a relative error of at most 0.012.
Values may be sent and summed in bfloat16 or wider, within the bound.
A program may use at most 64 MiB of HBM per device.

```python
import math
import jax
import jax.numpy as jnp
import numpy as np
from jax import lax

QUERY_HEADS = 32
KEY_VALUE_HEADS = 4
HEAD_SIZE = 128
WINDOW_LIMIT = 256
CONTEXT_TOKENS = 4096
NDOC = 8


def draw_queries(key, part):
    sampled_values = jax.random.truncated_normal(jax.random.fold_in(key, 3), -5.0, 5.0, (CONTEXT_TOKENS, QUERY_HEADS * HEAD_SIZE), jnp.float32)
    return sampled_values.astype(jnp.bfloat16)


def draw_key_matrix(key, part):
    sampled_values = jax.random.truncated_normal(jax.random.fold_in(key, 4), -5.0, 5.0, (CONTEXT_TOKENS, KEY_VALUE_HEADS * HEAD_SIZE), jnp.float32)
    return sampled_values.astype(jnp.bfloat16)


def draw_windows(key, part):
    drawn = jax.random.randint(jax.random.fold_in(key, 7), (QUERY_HEADS,), WINDOW_LIMIT // 8, WINDOW_LIMIT + 1)
    widest = jax.random.randint(jax.random.fold_in(key, 8), (), 0, QUERY_HEADS)
    return jnp.where(jnp.arange(QUERY_HEADS) == widest, WINDOW_LIMIT, drawn).astype(jnp.int32)


def block_levels(key, extent, cuts, least, high):
    gain, own = 1.0, jax.random.fold_in(key, 6)
    for dim, parts in cuts:
        draws = jnp.exp(jax.random.uniform(jax.random.fold_in(own, dim), (parts,), jnp.float32, least / len(cuts), high / len(cuts)))
        gain = gain * jnp.repeat(draws, extent[dim] // parts).reshape([-1 if axis == dim else 1 for axis in range(len(extent))])
    return gain


def length_profile(number_of, total, bound, slope):
    portions = [(1 << 20) // math.isqrt(rank ** slope) + 1 for rank in range(2, number_of + 1)]
    rest, counts = total - bound - (number_of - 1), [1] * (number_of - 1)
    while rest > 0:
        candidates = [i for i in range(number_of - 1) if counts[i] < bound]
        whole, left = sum([portions[i] for i in candidates]), rest
        for i in candidates:
            more = min(bound - counts[i], max(1, left * portions[i] // whole), rest)
            counts[i] = counts[i] + more
            rest = rest - more
    return np.array([bound] + counts)


def uneven_parts(key, count, total, reach, slope):
    if count == 2:
        one = jax.random.randint(key, (), max(1, total - reach), min(reach, total - 1) + 1)
        return jnp.stack([one, total - one])
    lengths = jnp.asarray(length_profile(count, total, reach, slope), jnp.int32)
    twos = (count - 1) // 2
    donor, taker = lengths[1:1 + 2 * twos:2], lengths[2:2 + 2 * twos:2]
    margin = jnp.minimum(donor - 1, reach - taker)
    moved = jax.random.randint(jax.random.fold_in(key, 1), (twos,), 0, 1 << 20) % (margin + 1)
    lengths = lengths.at[1:1 + 2 * twos:2].set(donor - moved).at[2:2 + 2 * twos:2].set(taker + moved)
    return lengths[jax.random.permutation(jax.random.fold_in(key, 2), count)]


def normal_values(own_key, extent, width, limit, cuts=(), held_as=jnp.bfloat16):
    entries = jax.random.normal(own_key, extent, jnp.float32) * width
    if len(cuts) > 0:
        entries = block_levels(own_key, extent, cuts, -0.22, 0.18) * entries
    return jnp.clip(entries, min=-limit, max=limit).astype(held_as)


def setup_inputs(seed: int = 0) -> dict:
    seeds = jax.random.split(jax.random.key(seed), 7)
    return {
        "queries": draw_queries(jax.random.fold_in(seeds[6], 71), 0),
        "key_matrix": draw_key_matrix(jax.random.fold_in(seeds[6], 71), 0),
        "value_matrix": normal_values(seeds[2], (CONTEXT_TOKENS, KEY_VALUE_HEADS * HEAD_SIZE), 1.0, 6.0, ((0, 32),)),
        "output_gradient": normal_values(seeds[3], (CONTEXT_TOKENS, QUERY_HEADS * HEAD_SIZE), 1.0, 6.0, ((0, 32),)),
        "doc_lengths": uneven_parts(seeds[4], NDOC, CONTEXT_TOKENS, 8 * WINDOW_LIMIT, 2).astype(jnp.int32),
        "windows": draw_windows(jax.random.fold_in(seeds[6], 71), 0),
    }


NEG_FILL = -1e+30

def doc_begin(positions, doc_lengths):
    doc_ends = jnp.cumsum(doc_lengths).astype(jnp.int32)
    doc_starts = (doc_ends - doc_lengths).astype(jnp.int32)
    inside = (positions[:, None] >= doc_starts[None, :]) & (positions[:, None] < doc_ends[None, :])
    return lax.optimization_barrier(jnp.sum(jnp.where(inside, doc_starts[None, :], 0), axis=1)).astype(jnp.int32)

def attend(query_rows, gradout_rows, key_tile_block, value_tile_block, query_pos, key_pos, begin_pos, row_limits):
    scale_factor = 1.0 / math.sqrt(query_rows.shape[-1])
    query_f = query_rows.astype(jnp.float32)
    gradout_f = gradout_rows.astype(jnp.float32)
    key_f = key_tile_block.astype(jnp.float32)
    value_f = value_tile_block.astype(jnp.float32)
    scores = jnp.einsum('qghd,kgd->ghqk', query_f, key_f) * scale_factor
    offsets = query_pos[:, None] - key_pos[None, :]
    inside_doc = (key_pos[None, :] >= begin_pos[:, None]) & (offsets >= 0)
    allowed = inside_doc[None, None] & (offsets[None, None] < row_limits[:, :, None, None])
    scores = jnp.where(allowed, scores, NEG_FILL)
    row_max = lax.optimization_barrier(jnp.max(scores, axis=-1, keepdims=True))
    shifted = jnp.exp(scores - row_max)
    probs = shifted / lax.optimization_barrier(jnp.sum(shifted, axis=-1, keepdims=True))
    probs_low = probs.astype(jnp.bfloat16)
    attn_out = jnp.einsum('ghqk,kgd->qghd', probs_low.astype(jnp.float32), value_f).astype(jnp.bfloat16)
    attn_out = lax.optimization_barrier(attn_out)
    delta_rows = lax.optimization_barrier(jnp.sum(gradout_f * attn_out.astype(jnp.float32), axis=-1))
    dprob = jnp.einsum('qghd,kgd->ghqk', gradout_f, value_f)
    dscore = (probs * (dprob - jnp.transpose(delta_rows, (1, 2, 0))[..., None]) * scale_factor).astype(jnp.bfloat16)
    dscore_f = dscore.astype(jnp.float32)
    dquery = jnp.einsum('ghqk,kgd->qghd', dscore_f, key_f).astype(jnp.bfloat16)
    key_gradient = jnp.einsum('ghqk,qghd->kgd', dscore_f, query_f)
    return (dquery, key_gradient)

def reference(queries, key_matrix, value_matrix, output_gradient, doc_lengths, windows):
    group_width = QUERY_HEADS // KEY_VALUE_HEADS
    block_count = CONTEXT_TOKENS // WINDOW_LIMIT
    margin_width = jnp.zeros((WINDOW_LIMIT, KEY_VALUE_HEADS * HEAD_SIZE), jnp.bfloat16)
    key_with_margin = jnp.concatenate([margin_width, key_matrix], axis=0)
    value_with_margin = jnp.concatenate([margin_width, value_matrix], axis=0)
    row_limits = windows.reshape(KEY_VALUE_HEADS, group_width)

    def advance(key_running_sum, block_index):
        leading_row = (block_index * WINDOW_LIMIT).astype(jnp.int32)
        query_tile_block = lax.dynamic_slice_in_dim(queries, leading_row, WINDOW_LIMIT, 0).reshape(WINDOW_LIMIT, KEY_VALUE_HEADS, group_width, HEAD_SIZE)
        output_gradient_block = lax.dynamic_slice_in_dim(output_gradient, leading_row, WINDOW_LIMIT, 0).reshape(WINDOW_LIMIT, KEY_VALUE_HEADS, group_width, HEAD_SIZE)
        key_tile_block = lax.dynamic_slice_in_dim(key_with_margin, leading_row, 2 * WINDOW_LIMIT, 0).reshape(2 * WINDOW_LIMIT, KEY_VALUE_HEADS, HEAD_SIZE)
        value_tile_block = lax.dynamic_slice_in_dim(value_with_margin, leading_row, 2 * WINDOW_LIMIT, 0).reshape(2 * WINDOW_LIMIT, KEY_VALUE_HEADS, HEAD_SIZE)
        query_pos = (leading_row + jnp.arange(WINDOW_LIMIT, dtype=jnp.int32)).astype(jnp.int32)
        key_pos = (leading_row - WINDOW_LIMIT + jnp.arange(2 * WINDOW_LIMIT, dtype=jnp.int32)).astype(jnp.int32)
        begin_pos = doc_begin(query_pos, doc_lengths)
        dquery, key_gradient = attend(query_tile_block, output_gradient_block, key_tile_block, value_tile_block, query_pos, key_pos, begin_pos, row_limits)
        key_portion = lax.dynamic_slice_in_dim(key_running_sum, leading_row, 2 * WINDOW_LIMIT, 0) + key_gradient.reshape(2 * WINDOW_LIMIT, KEY_VALUE_HEADS * HEAD_SIZE)
        key_running_sum = lax.dynamic_update_slice_in_dim(key_running_sum, key_portion, leading_row, 0)
        return (key_running_sum, dquery.reshape(WINDOW_LIMIT, QUERY_HEADS * HEAD_SIZE))
    empty_running_sum = jnp.zeros((WINDOW_LIMIT + CONTEXT_TOKENS, KEY_VALUE_HEADS * HEAD_SIZE), jnp.float32)
    key_running_sum, dq_blocks = lax.scan(advance, empty_running_sum, jnp.arange(block_count, dtype=jnp.int32))
    query_grad = dq_blocks.reshape(CONTEXT_TOKENS, QUERY_HEADS * HEAD_SIZE)
    return (query_grad, key_running_sum[WINDOW_LIMIT:].astype(jnp.bfloat16))
```

```python
import functools
import math

import jax
import jax.numpy as jnp
from jax import lax
from jax.experimental import pallas as pl
from jax.experimental.pallas import tpu as pltpu
from jax.sharding import PartitionSpec as P

QUERY_HEADS = 32
KEY_VALUE_HEADS = 4
HEAD_SIZE = 128
WINDOW_LIMIT = 256

NEG_FILL = -1e30
MESH = pl.DeviceIdType.MESH
PAIR = 2
HALO = 2
AHEAD = 2


def attention_kernel(
    ctx_count,
    hs_count,
    rows,
    doc_ref,
    win_ref,
    q_hbm,
    k_hbm,
    v_hbm,
    do_hbm,
    dq_ref,
    dk_ref,
    q_ref,
    do_ref,
    kx_ref,
    vx_ref,
    own_ref,
    ds_ref,
    qs_ref,
    out_buf,
    in_buf,
    local_sem,
    fs_sem,
    fr_sem,
    bs_sem,
    br_sem,
):
    group = QUERY_HEADS // KEY_VALUE_HEADS
    group_cols = group * HEAD_SIZE
    c, z = lax.axis_index("ctx"), lax.axis_index("hs")
    place = c * hs_count + z
    total = ctx_count * hs_count
    edge = HALO * rows
    ext = edge + rows

    after = place + 1 < total
    sends_on = ((z >= 2) & (z <= hs_count - 2)) | ((z == 0) & (c > 0))
    joins = (z >= 3) | ((z == 1) & (c > 0))

    def at(step):
        index = place + step
        return (lax.div(index, hs_count), lax.rem(index, hs_count))

    def cols(g):
        return pl.ds(pl.multiple_of(g * HEAD_SIZE, HEAD_SIZE), HEAD_SIZE)

    def wide(g):
        return pl.ds(pl.multiple_of(g * group_cols, group_cols), group_cols)

    def loads(g):
        return (
            pltpu.make_async_copy(q_hbm.at[:, wide(g)], q_ref.at[:, wide(g)], local_sem.at[0, g]),
            pltpu.make_async_copy(
                do_hbm.at[:, wide(g)], do_ref.at[:, wide(g)], local_sem.at[1, g]
            ),
            pltpu.make_async_copy(
                k_hbm.at[:, cols(g)], kx_ref.at[pl.ds(edge, rows), cols(g)], local_sem.at[2, g]
            ),
            pltpu.make_async_copy(
                v_hbm.at[:, cols(g)], vx_ref.at[pl.ds(edge, rows), cols(g)], local_sem.at[3, g]
            ),
        )

    def block_rows(slot):
        return pl.ds(edge - slot * rows, rows)

    def forward(kind, g, source, slot):
        pairs = ((k_hbm, kx_ref), (v_hbm, vx_ref))
        return tuple(
            pltpu.make_async_remote_copy(
                src_ref=src.at[:, cols(g)] if source == 0 else dst.at[block_rows(source), cols(g)],
                dst_ref=dst.at[block_rows(slot), cols(g)],
                send_sem=fs_sem.at[i, kind, g],
                recv_sem=fr_sem.at[i, slot - 1, g],
                device_id=at(1),
                device_id_type=MESH,
            )
            for i, (src, dst) in enumerate(pairs)
        )

    own_next = lambda g: forward(0, g, 0, 1)
    pass_on = lambda g: forward(1, g, 1, 2)

    def backward(g, part, target, step):
        return pltpu.make_async_remote_copy(
            src_ref=out_buf.at[part, :, cols(g)],
            dst_ref=in_buf.at[target, :, cols(g)],
            send_sem=bs_sem.at[part, g],
            recv_sem=br_sem.at[target, g],
            device_id=at(step),
            device_id_type=MESH,
        )

    def start(copies):
        for copy in copies:
            copy.start()

    def received(copies):
        for copy in copies:
            copy.wait_recv()

    def sent(copies):
        for copy in copies:
            copy.wait_send()

    barrier = pltpu.get_barrier_semaphore()

    @pl.when(place >= 1)
    def _():
        pl.semaphore_signal(barrier, inc=1, device_id=at(-1), device_id_type=MESH)

    @pl.loop(0, KEY_VALUE_HEADS)
    def _(g):
        start(loads(g))

    for slot in range(1, HALO + 1):

        @pl.when(place < slot)
        def _():
            kx_ref[block_rows(slot), :] = jnp.zeros((rows, kx_ref.shape[1]), kx_ref.dtype)
            vx_ref[block_rows(slot), :] = jnp.zeros((rows, vx_ref.shape[1]), vx_ref.dtype)

    @pl.when(after)
    def _():
        pl.semaphore_wait(barrier, 1)

    def send(g):
        @pl.when(after & (g < KEY_VALUE_HEADS))
        def _():
            start(own_next(g))

    ahead = jnp.where(z == 0, KEY_VALUE_HEADS, AHEAD)
    pl.loop(0, ahead)(send)

    def relay(g):
        @pl.when(place >= 1)
        def _():
            received(own_next(g))

        @pl.when(after & (place >= 1))
        def _():
            start(pass_on(g))

        send(g + ahead)

    first = jnp.where(z == 1, KEY_VALUE_HEADS, 1)
    pl.loop(0, first)(relay)

    base = place * rows
    query_off = lax.broadcasted_iota(jnp.int32, (1, rows), 1)
    query_pos = query_off + base

    def doc_step(n, carry):
        start, begin = carry
        begin = jnp.where(query_pos >= start, start, begin)
        return start + doc_ref[n], begin

    _, begin = lax.fori_loop(
        0, doc_ref.shape[0], doc_step, (jnp.int32(0), jnp.zeros((1, rows), jnp.int32))
    )
    begin_rel = begin - base + edge

    scale = 1.0 / math.sqrt(HEAD_SIZE)
    scale2 = scale * math.log2(math.e)
    key_off = lax.broadcasted_iota(jnp.int32, (rows, PAIR * rows), 0)
    causal = key_off <= jnp.concatenate([query_off] * PAIR, axis=1)

    def take(total_ref, source, g):
        backward(g, 0, source, -1).wait_recv()
        total_ref[:, cols(g)] = (
            total_ref[:, cols(g)].astype(jnp.float32) + in_buf[source, :, cols(g)].astype(jnp.float32)
        ).astype(total_ref.dtype)

    def join(g):
        take(out_buf.at[1], 2, g)

        @pl.when(place >= 2)
        def _():
            backward(g, 1, 1, -2).start()

    @pl.loop(0, KEY_VALUE_HEADS)
    def _(g):
        for copy in loads(g):
            copy.wait()

        @pl.when((z != 1) & (g + 1 < KEY_VALUE_HEADS))
        def _():
            relay(g + 1)

        @pl.when(place >= 2)
        def _():
            received(pass_on(g))

        keys = kx_ref[:, cols(g)]
        values = vx_ref[:, cols(g)]
        keys_t = keys.astype(jnp.float32).T.astype(jnp.bfloat16)
        for pair in range(group // PAIR):
            heads = [g * group + pair * PAIR + n for n in range(PAIR)]
            queries = jnp.concatenate([q_ref[:, cols(h)] for h in heads], axis=0)
            gradout = jnp.concatenate([do_ref[:, cols(h)] for h in heads], axis=0)
            lowest = jnp.concatenate(
                [jnp.maximum(begin_rel, query_off + (edge + 1) - win_ref[h]) for h in heads],
                axis=1,
            )
            dims = (((1,), (1,)), ((), ()))
            tiles = []
            row_max = None
            for t in range(ext // rows):
                tile = lax.dot_general(
                    keys[t * rows : (t + 1) * rows], queries, dims, preferred_element_type=jnp.float32
                )
                allowed = key_off >= lowest - t * rows
                if t == ext // rows - 1:
                    allowed = allowed & causal
                tile = jnp.where(allowed, tile, NEG_FILL)
                top = jnp.max(tile, axis=0, keepdims=True)
                row_max = top if row_max is None else jnp.maximum(row_max, top)
                tiles.append(tile)
            total_sum, total_dot = 0.0, 0.0
            parts = []
            for t, tile in enumerate(tiles):
                shifted = jnp.exp2((tile - row_max) * scale2)
                dprob = lax.dot_general(
                    values[t * rows : (t + 1) * rows], gradout, dims, preferred_element_type=jnp.float32
                )
                total_sum = total_sum + jnp.sum(shifted, axis=0, keepdims=True)
                total_dot = total_dot + jnp.sum(shifted * dprob, axis=0, keepdims=True)
                parts.append((shifted, dprob))
            inverse = 1.0 / total_sum
            delta = total_dot * inverse
            factor = inverse * scale
            dscore = jnp.concatenate(
                [((s * factor) * (d - delta)).astype(jnp.bfloat16) for s, d in parts], axis=0
            )
            ds_ref[:, pair * PAIR * rows : (pair + 1) * PAIR * rows] = dscore
            qs_ref[pair * PAIR * rows : (pair + 1) * PAIR * rows, :] = queries

        dkx = lax.dot_general(
            ds_ref[...], qs_ref[...], (((1,), (0,)), ((), ())), preferred_element_type=jnp.float32
        )
        own_ref[:, cols(g)] = dkx[edge:]
        out_buf[0, :, cols(g)] = dkx[rows:edge].astype(jnp.bfloat16)
        out_buf[1, :, cols(g)] = dkx[:rows].astype(jnp.bfloat16)

        @pl.when(sends_on)
        def _():
            backward(g, 0, 2, 1).start()

        @pl.when(jnp.logical_not(sends_on) & (place >= 1))
        def _():
            backward(g, 0, 0, -1).start()

        @pl.when(jnp.logical_not(joins) & (place >= 2))
        def _():
            backward(g, 1, 1, -2).start()

        @pl.when(joins & (g >= 1))
        def _():
            join(g - 1)

        for pair in range(group // PAIR):
            dq_t = lax.dot_general(
                keys_t,
                ds_ref[:, pair * PAIR * rows : (pair + 1) * PAIR * rows],
                (((1,), (0,)), ((), ())),
                preferred_element_type=jnp.float32,
            )
            for n in range(PAIR):
                h = g * group + pair * PAIR + n
                dq_ref[:, cols(h)] = dq_t[:, n * rows : (n + 1) * rows].T.astype(jnp.bfloat16)

    @pl.when(joins)
    def _():
        join(KEY_VALUE_HEADS - 1)

    @pl.loop(0, KEY_VALUE_HEADS)
    def _(g):
        @pl.when((z == 0) | (z == hs_count - 2))
        def _():
            take(own_ref, 0, g)

        @pl.when(place + 2 < total)
        def _():
            take(own_ref, 1, g)

        dk_ref[:, cols(g)] = own_ref[:, cols(g)].astype(jnp.bfloat16)

    @pl.loop(0, KEY_VALUE_HEADS)
    def _(g):
        for there, copies in ((after, own_next), (after & (place >= 1), pass_on)):

            @pl.when(there)
            def _():
                sent(copies(g))

        @pl.when(place >= 1)
        def _():
            backward(g, 0, 0, -1).wait_send()

        @pl.when(place >= 2)
        def _():
            backward(g, 1, 1, -2).wait_send()


def shards(queries, key_matrix, value_matrix, output_gradient, doc_lengths, windows):
    rows = queries.shape[0]
    ctx_count, hs_count = lax.axis_size("ctx"), lax.axis_size("hs")
    if HALO * rows < WINDOW_LIMIT - 1 or hs_count < 3:
        raise ValueError("unsupported shape")
    groups = KEY_VALUE_HEADS
    ext = (HALO + 1) * rows
    kv_cols = key_matrix.shape[1]
    any_spec = pl.BlockSpec(memory_space=pltpu.HBM)
    smem_spec = pl.BlockSpec(memory_space=pltpu.SMEM)
    return pl.pallas_call(
        functools.partial(attention_kernel, ctx_count, hs_count, rows),
        out_shape=(
            pltpu.VMEM(queries.shape, jnp.bfloat16),
            pltpu.VMEM(key_matrix.shape, jnp.bfloat16),
        ),
        in_specs=[smem_spec, smem_spec, any_spec, any_spec, any_spec, any_spec],
        out_specs=(pl.BlockSpec(memory_space=pltpu.VMEM), pl.BlockSpec(memory_space=pltpu.VMEM)),
        scratch_shapes=[
            pltpu.VMEM(queries.shape, jnp.bfloat16),
            pltpu.VMEM(queries.shape, jnp.bfloat16),
            pltpu.VMEM((ext, kv_cols), jnp.bfloat16),
            pltpu.VMEM((ext, kv_cols), jnp.bfloat16),
            pltpu.VMEM((rows, kv_cols), jnp.float32),
            pltpu.VMEM((ext, QUERY_HEADS // KEY_VALUE_HEADS * rows), jnp.bfloat16),
            pltpu.VMEM((QUERY_HEADS // KEY_VALUE_HEADS * rows, HEAD_SIZE), jnp.bfloat16),
            pltpu.VMEM((2, rows, kv_cols), jnp.bfloat16),
            pltpu.VMEM((3, rows, kv_cols), jnp.bfloat16),
            pltpu.SemaphoreType.DMA((4, groups)),
            pltpu.SemaphoreType.DMA((2, 2, groups)),
            pltpu.SemaphoreType.DMA((2, HALO, groups)),
            pltpu.SemaphoreType.DMA((2, groups)),
            pltpu.SemaphoreType.DMA((3, groups)),
        ],
        compiler_params=pltpu.CompilerParams(collective_id=0, has_side_effects=True),
    )(doc_lengths, windows, queries, key_matrix, value_matrix, output_gradient)


def solution(mesh):
    spec = P(("ctx", "hs"), None)
    return jax.shard_map(
        shards,
        mesh=mesh,
        in_specs=(spec, spec, spec, spec, P(), P()),
        out_specs=(spec, spec),
        check_vma=False,
    )
```

```python
import functools
import math

import jax
import jax.numpy as jnp
from jax import lax
from jax.experimental import pallas as pl
from jax.experimental.pallas import tpu as pltpu
from jax.sharding import PartitionSpec as P

QUERY_HEADS = 32
KEY_VALUE_HEADS = 4
HEAD_SIZE = 128
WINDOW_LIMIT = 256

NEG_FILL = -1e30
MESH = pl.DeviceIdType.MESH
PAIR = 2
HALO = 2
AHEAD = 2
DIRECT = 1
WRAP = 2


def attention_kernel(
    ctx_count,
    hs_count,
    rows,
    doc_hbm,
    win_hbm,
    q_hbm,
    k_hbm,
    v_hbm,
    do_hbm,
    dq_ref,
    dk_ref,
    doc_ref,
    win_ref,
    q_ref,
    do_ref,
    kx_ref,
    vx_ref,
    own_ref,
    ds_ref,
    qs_ref,
    out_buf,
    in_buf,
    table_sem,
    local_sem,
    fs_sem,
    fr_sem,
    bs_sem,
    br_sem,
):
    group = QUERY_HEADS // KEY_VALUE_HEADS
    group_cols = group * HEAD_SIZE
    c, z = lax.axis_index("ctx"), lax.axis_index("hs")
    place = c * hs_count + z
    total = ctx_count * hs_count
    edge = HALO * rows
    ext = edge + rows

    after = place + 1 < total
    sends_on = ((z >= 2) & (z <= hs_count - 2)) | ((z == 0) & (c > 0))
    joins = (z >= 3) | ((z == 1) & (c > 0))

    def at(step):
        index = place + step
        return (lax.div(index, hs_count), lax.rem(index, hs_count))

    def cols(g):
        return pl.ds(pl.multiple_of(g * HEAD_SIZE, HEAD_SIZE), HEAD_SIZE)

    def wide(g):
        return pl.ds(pl.multiple_of(g * group_cols, group_cols), group_cols)

    def rows_of(g):
        return (
            pltpu.make_async_copy(q_hbm.at[:, wide(g)], q_ref.at[:, wide(g)], local_sem.at[0, g]),
            pltpu.make_async_copy(
                do_hbm.at[:, wide(g)], do_ref.at[:, wide(g)], local_sem.at[1, g]
            ),
        )

    def keys_of(g):
        return (
            pltpu.make_async_copy(
                k_hbm.at[:, cols(g)], kx_ref.at[pl.ds(edge, rows), cols(g)], local_sem.at[2, g]
            ),
            pltpu.make_async_copy(
                v_hbm.at[:, cols(g)], vx_ref.at[pl.ds(edge, rows), cols(g)], local_sem.at[3, g]
            ),
        )

    def block_rows(slot):
        return pl.ds(edge - slot * rows, rows)

    def forward(kind, g, source, slot):
        pairs = ((k_hbm, kx_ref), (v_hbm, vx_ref))
        return tuple(
            pltpu.make_async_remote_copy(
                src_ref=src.at[:, cols(g)] if source == 0 else dst.at[block_rows(source), cols(g)],
                dst_ref=dst.at[block_rows(slot), cols(g)],
                send_sem=fs_sem.at[i, kind, g],
                recv_sem=fr_sem.at[i, slot - 1, g],
                device_id=at(1),
                device_id_type=MESH,
            )
            for i, (src, dst) in enumerate(pairs)
        )

    own_next = lambda g: forward(0, g, 0, 1)
    pass_on = lambda g: forward(1, g, 1, 2)

    def backward(g, part, target, step):
        return pltpu.make_async_remote_copy(
            src_ref=out_buf.at[part, :, cols(g)],
            dst_ref=in_buf.at[target, :, cols(g)],
            send_sem=bs_sem.at[part, g],
            recv_sem=br_sem.at[target, g],
            device_id=at(step),
            device_id_type=MESH,
        )

    def start(copies):
        for copy in copies:
            copy.start()

    def received(copies):
        for copy in copies:
            copy.wait_recv()

    def sent(copies):
        for copy in copies:
            copy.wait_send()

    barrier = pltpu.get_barrier_semaphore()

    @pl.when(place >= 1)
    def _():
        pl.semaphore_signal(barrier, inc=1, device_id=at(-1), device_id_type=MESH)

    tables = (
        pltpu.make_async_copy(doc_hbm, doc_ref, table_sem.at[0]),
        pltpu.make_async_copy(win_hbm, win_ref, table_sem.at[1]),
    )

    for slot in range(1, HALO + 1):

        @pl.when(place < slot)
        def _():
            kx_ref[block_rows(slot), :] = jnp.zeros((rows, kx_ref.shape[1]), kx_ref.dtype)
            vx_ref[block_rows(slot), :] = jnp.zeros((rows, vx_ref.shape[1]), vx_ref.dtype)

    @pl.when(after)
    def _():
        pl.semaphore_wait(barrier, 1)

    def send(g):
        @pl.when(after & (g < KEY_VALUE_HEADS))
        def _():
            start(own_next(g))

    ahead = jnp.where(z == 0, KEY_VALUE_HEADS, AHEAD)
    pl.loop(0, ahead)(send)
    start(tables)

    @pl.loop(0, KEY_VALUE_HEADS)
    def _(g):
        start(keys_of(g) + rows_of(g))

    def relay(g):
        @pl.when(place >= 1)
        def _():
            received(own_next(g))

        @pl.when(after & (place >= 1))
        def _():
            start(pass_on(g))

        send(g + ahead)

    first = jnp.where(z == 1, KEY_VALUE_HEADS, 1)
    pl.loop(0, first)(relay)

    for copy in tables:
        copy.wait()

    base = place * rows
    query_off = lax.broadcasted_iota(jnp.int32, (1, rows), 1)
    query_pos = query_off + base

    def doc_step(n, carry):
        start, begin = carry
        begin = jnp.where(query_pos >= start, start, begin)
        return start + doc_ref[n], begin

    _, begin = lax.fori_loop(
        0, doc_ref.shape[0], doc_step, (jnp.int32(0), jnp.zeros((1, rows), jnp.int32))
    )
    begin_rel = begin - base + edge

    scale = 1.0 / math.sqrt(HEAD_SIZE)
    scale2 = scale * math.log2(math.e)
    key_off = lax.broadcasted_iota(jnp.int32, (rows, PAIR * rows), 0)
    causal = key_off <= jnp.concatenate([query_off] * PAIR, axis=1)
    own_or_far = jnp.where(causal, key_off + edge, key_off)
    own_part = jnp.where(causal, 1.0, 0.0).astype(jnp.bfloat16)

    def take(total_ref, source, g):
        backward(g, 0, source, -1).wait_recv()
        total_ref[:, cols(g)] = (
            total_ref[:, cols(g)].astype(jnp.float32) + in_buf[source, :, cols(g)].astype(jnp.float32)
        ).astype(total_ref.dtype)

    def straight(g):
        return g >= KEY_VALUE_HEADS - jnp.where(z <= 1, WRAP, DIRECT)

    def join(g):
        take(out_buf.at[1], 2, g)

        @pl.when(place >= 2)
        def _():
            backward(g, 1, 1, -2).start()

    @pl.loop(0, KEY_VALUE_HEADS)
    def _(g):
        for copy in keys_of(g) + rows_of(g):
            copy.wait()

        @pl.when((z != 1) & (g + 1 < KEY_VALUE_HEADS))
        def _():
            relay(g + 1)

        @pl.when(place >= 2)
        def _():
            received(pass_on(g))

        keys = kx_ref[:, cols(g)]
        values = vx_ref[:, cols(g)]
        keys_t = keys.astype(jnp.float32).T.astype(jnp.bfloat16)
        for pair in range(group // PAIR):
            heads = [g * group + pair * PAIR + n for n in range(PAIR)]
            queries = jnp.concatenate([q_ref[:, cols(h)] for h in heads], axis=0)
            gradout = jnp.concatenate([do_ref[:, cols(h)] for h in heads], axis=0)
            lowest = jnp.concatenate(
                [jnp.maximum(begin_rel, query_off + (edge + 1) - win_ref[h]) for h in heads],
                axis=1,
            )
            def against(block):
                far, near, own = (
                    lax.dot_general(
                        block[t * rows : (t + 1) * rows],
                        other,
                        (((1,), (1,)), ((), ())),
                        preferred_element_type=jnp.float32,
                    )
                    for t in range(HALO + 1)
                )
                return jnp.where(causal, own, far), near

            other = queries
            outer, inner = against(keys)
            outer = jnp.where(own_or_far >= lowest, outer, NEG_FILL)
            inner = jnp.where(key_off >= lowest - rows, inner, NEG_FILL)
            row_max = jnp.max(jnp.maximum(outer, inner), axis=0, keepdims=True)
            outer = jnp.exp2((outer - row_max) * scale2)
            inner = jnp.exp2((inner - row_max) * scale2)
            other = gradout
            outer_d, inner_d = against(values)
            inverse = 1.0 / jnp.sum(outer + inner, axis=0, keepdims=True)
            delta = jnp.sum(outer * outer_d + inner * inner_d, axis=0, keepdims=True) * inverse
            factor = inverse * scale
            outer = ((outer * factor) * (outer_d - delta)).astype(jnp.bfloat16)
            inner = ((inner * factor) * (inner_d - delta)).astype(jnp.bfloat16)
            own = outer * own_part
            lanes = slice(pair * PAIR * rows, (pair + 1) * PAIR * rows)
            ds_ref[:rows, lanes] = outer - own
            ds_ref[rows:edge, lanes] = inner
            ds_ref[edge:, lanes] = own
            qs_ref[pair * PAIR * rows : (pair + 1) * PAIR * rows, :] = queries

        dkx = lax.dot_general(
            ds_ref[...], qs_ref[...], (((1,), (0,)), ((), ())), preferred_element_type=jnp.float32
        )
        own_ref[:, cols(g)] = dkx[edge:]
        out_buf[0, :, cols(g)] = dkx[rows:edge].astype(jnp.bfloat16)
        out_buf[1, :, cols(g)] = dkx[:rows].astype(jnp.bfloat16)

        @pl.when(sends_on & jnp.logical_not(straight(g)))
        def _():
            backward(g, 0, 2, 1).start()

        @pl.when((straight(g) | jnp.logical_not(sends_on)) & (place >= 1))
        def _():
            backward(g, 0, 0, -1).start()

        @pl.when((straight(g) | jnp.logical_not(joins)) & (place >= 2))
        def _():
            backward(g, 1, 1, -2).start()

        @pl.when(joins & (g >= 1) & jnp.logical_not(straight(g - 1)))
        def _():
            join(g - 1)

        for pair in range(group // PAIR):
            dq_t = lax.dot_general(
                keys_t,
                ds_ref[:, pair * PAIR * rows : (pair + 1) * PAIR * rows],
                (((1,), (0,)), ((), ())),
                preferred_element_type=jnp.float32,
            )
            for n in range(PAIR):
                h = g * group + pair * PAIR + n
                dq_ref[:, cols(h)] = dq_t[:, n * rows : (n + 1) * rows].T.astype(jnp.bfloat16)

    @pl.loop(0, KEY_VALUE_HEADS)
    def _(g):
        @pl.when((z == 0) | (z == hs_count - 2) | ((g >= KEY_VALUE_HEADS - jnp.where(z == hs_count - 1, WRAP, DIRECT)) & after))
        def _():
            take(own_ref, 0, g)

        @pl.when(place + 2 < total)
        def _():
            take(own_ref, 1, g)

        dk_ref[:, cols(g)] = own_ref[:, cols(g)].astype(jnp.bfloat16)

    @pl.loop(0, KEY_VALUE_HEADS)
    def _(g):
        for there, copies in ((after, own_next), (after & (place >= 1), pass_on)):

            @pl.when(there)
            def _():
                sent(copies(g))

        @pl.when(place >= 1)
        def _():
            backward(g, 0, 0, -1).wait_send()

        @pl.when(place >= 2)
        def _():
            backward(g, 1, 1, -2).wait_send()


def store_kernel(dq_ref, dk_ref, dq_hbm, dk_hbm, sem):
    copies = (
        pltpu.make_async_copy(dq_ref, dq_hbm, sem.at[0]),
        pltpu.make_async_copy(dk_ref, dk_hbm, sem.at[1]),
    )
    for copy in copies:
        copy.start()
    for copy in copies:
        copy.wait()


def shards(queries, key_matrix, value_matrix, output_gradient, doc_lengths, windows):
    rows = queries.shape[0]
    ctx_count, hs_count = lax.axis_size("ctx"), lax.axis_size("hs")
    if HALO * rows < WINDOW_LIMIT or hs_count < 3:
        raise ValueError("unsupported shape")
    groups = KEY_VALUE_HEADS
    ext = (HALO + 1) * rows
    kv_cols = key_matrix.shape[1]
    any_spec = pl.BlockSpec(memory_space=pltpu.HBM)
    grads = pl.pallas_call(
        functools.partial(attention_kernel, ctx_count, hs_count, rows),
        out_shape=(
            pltpu.VMEM(queries.shape, jnp.bfloat16),
            pltpu.VMEM(key_matrix.shape, jnp.bfloat16),
        ),
        in_specs=[any_spec, any_spec, any_spec, any_spec, any_spec, any_spec],
        out_specs=(pl.BlockSpec(memory_space=pltpu.VMEM), pl.BlockSpec(memory_space=pltpu.VMEM)),
        scratch_shapes=[
            pltpu.SMEM(doc_lengths.shape, jnp.int32),
            pltpu.SMEM(windows.shape, jnp.int32),
            pltpu.VMEM(queries.shape, jnp.bfloat16),
            pltpu.VMEM(queries.shape, jnp.bfloat16),
            pltpu.VMEM((ext, kv_cols), jnp.bfloat16),
            pltpu.VMEM((ext, kv_cols), jnp.bfloat16),
            pltpu.VMEM((rows, kv_cols), jnp.float32),
            pltpu.VMEM((ext, QUERY_HEADS // KEY_VALUE_HEADS * rows), jnp.bfloat16),
            pltpu.VMEM((QUERY_HEADS // KEY_VALUE_HEADS * rows, HEAD_SIZE), jnp.bfloat16),
            pltpu.VMEM((2, rows, kv_cols), jnp.bfloat16),
            pltpu.VMEM((3, rows, kv_cols), jnp.bfloat16),
            pltpu.SemaphoreType.DMA((2,)),
            pltpu.SemaphoreType.DMA((4, groups)),
            pltpu.SemaphoreType.DMA((2, 2, groups)),
            pltpu.SemaphoreType.DMA((2, HALO, groups)),
            pltpu.SemaphoreType.DMA((2, groups)),
            pltpu.SemaphoreType.DMA((3, groups)),
        ],
        compiler_params=pltpu.CompilerParams(collective_id=0, has_side_effects=True),
    )(doc_lengths, windows, queries, key_matrix, value_matrix, output_gradient)
    vmem_spec = pl.BlockSpec(memory_space=pltpu.VMEM)
    return pl.pallas_call(
        store_kernel,
        out_shape=(
            jax.ShapeDtypeStruct(queries.shape, jnp.bfloat16),
            jax.ShapeDtypeStruct(key_matrix.shape, jnp.bfloat16),
        ),
        in_specs=[pl.BlockSpec(memory_space=pl.ANY)] * 2,
        out_specs=(any_spec, any_spec),
        scratch_shapes=[pltpu.SemaphoreType.DMA((2,))],
        compiler_params=pltpu.CompilerParams(vmem_limit_bytes=2**20),
    )(*grads)


def solution(mesh):
    spec = P(("ctx", "hs"), None)
    return jax.shard_map(
        shards,
        mesh=mesh,
        in_specs=(spec, spec, spec, spec, P(), P()),
        out_specs=(spec, spec),
        check_vma=False,
    )
```

```python
import functools
import math

import jax
import jax.numpy as jnp
from jax import lax
from jax.experimental import pallas as pl
from jax.experimental.pallas import tpu as pltpu
from jax.sharding import PartitionSpec as P

QUERY_HEADS = 32
KEY_VALUE_HEADS = 4
HEAD_SIZE = 128
WINDOW_LIMIT = 256

NEG_FILL = -1e30
MESH = pl.DeviceIdType.MESH
PAIR = 2
HALO = 2
AHEAD = 2
DIRECT = 1


def attention_kernel(
    ctx_count,
    hs_count,
    rows,
    doc_hbm,
    win_hbm,
    q_hbm,
    k_hbm,
    v_hbm,
    do_hbm,
    dq_ref,
    dk_ref,
    doc_ref,
    win_ref,
    q_ref,
    do_ref,
    kx_ref,
    vx_ref,
    own_ref,
    ds_ref,
    qs_ref,
    out_buf,
    in_buf,
    table_sem,
    local_sem,
    fs_sem,
    fr_sem,
    bs_sem,
    br_sem,
):
    group = QUERY_HEADS // KEY_VALUE_HEADS
    group_cols = group * HEAD_SIZE
    c, z = lax.axis_index("ctx"), lax.axis_index("hs")
    place = c * hs_count + z
    total = ctx_count * hs_count
    edge = HALO * rows
    ext = edge + rows

    after = place + 1 < total
    last = z == hs_count - 1
    sends_on = ((z >= 2) & (z <= hs_count - 2)) | ((z == 0) & (c > 0))
    joins = (z >= 3) | ((z == 1) & (c > 0))

    def at(step):
        index = place + step
        return (lax.div(index, hs_count), lax.rem(index, hs_count))

    def cols(g):
        return pl.ds(pl.multiple_of(g * HEAD_SIZE, HEAD_SIZE), HEAD_SIZE)

    def wide(g):
        return pl.ds(pl.multiple_of(g * group_cols, group_cols), group_cols)

    def rows_of(g):
        return (
            pltpu.make_async_copy(q_hbm.at[:, wide(g)], q_ref.at[:, wide(g)], local_sem.at[0, g]),
            pltpu.make_async_copy(
                do_hbm.at[:, wide(g)], do_ref.at[:, wide(g)], local_sem.at[1, g]
            ),
        )

    def keys_of(g):
        return (
            pltpu.make_async_copy(
                k_hbm.at[:, cols(g)], kx_ref.at[pl.ds(edge, rows), cols(g)], local_sem.at[2, g]
            ),
            pltpu.make_async_copy(
                v_hbm.at[:, cols(g)], vx_ref.at[pl.ds(edge, rows), cols(g)], local_sem.at[3, g]
            ),
        )

    def block_rows(slot):
        return pl.ds(edge - slot * rows, rows)

    def forward(kind, g, source, slot):
        pairs = ((k_hbm, kx_ref), (v_hbm, vx_ref))
        return tuple(
            pltpu.make_async_remote_copy(
                src_ref=src.at[:, cols(g)] if source == 0 else dst.at[block_rows(source), cols(g)],
                dst_ref=dst.at[block_rows(slot), cols(g)],
                send_sem=fs_sem.at[i, kind, g],
                recv_sem=fr_sem.at[i, slot - 1, g],
                device_id=at(1),
                device_id_type=MESH,
            )
            for i, (src, dst) in enumerate(pairs)
        )

    own_next = lambda g: forward(0, g, 0, 1)
    pass_on = lambda g: forward(1, g, 1, 2)

    def backward(g, part, target, step):
        return pltpu.make_async_remote_copy(
            src_ref=out_buf.at[part, :, cols(g)],
            dst_ref=in_buf.at[target, :, cols(g)],
            send_sem=bs_sem.at[part, g],
            recv_sem=br_sem.at[target, g],
            device_id=at(step),
            device_id_type=MESH,
        )

    def start(copies):
        for copy in copies:
            copy.start()

    def received(copies):
        for copy in copies:
            copy.wait_recv()

    def sent(copies):
        for copy in copies:
            copy.wait_send()

    barrier = pltpu.get_barrier_semaphore()

    @pl.when(place >= 1)
    def _():
        pl.semaphore_signal(barrier, inc=1, device_id=at(-1), device_id_type=MESH)

    tables = (
        pltpu.make_async_copy(doc_hbm, doc_ref, table_sem.at[0]),
        pltpu.make_async_copy(win_hbm, win_ref, table_sem.at[1]),
    )

    for slot in range(1, HALO + 1):

        @pl.when(place < slot)
        def _():
            kx_ref[block_rows(slot), :] = jnp.zeros((rows, kx_ref.shape[1]), kx_ref.dtype)
            vx_ref[block_rows(slot), :] = jnp.zeros((rows, vx_ref.shape[1]), vx_ref.dtype)

    @pl.when(after)
    def _():
        pl.semaphore_wait(barrier, 1)

    def send(g):
        @pl.when(after & (g < KEY_VALUE_HEADS))
        def _():
            start(own_next(g))

    ahead = jnp.where(z == 0, KEY_VALUE_HEADS, AHEAD)
    pl.loop(0, ahead)(send)
    start(tables)

    @pl.loop(0, KEY_VALUE_HEADS)
    def _(g):
        start(keys_of(g) + rows_of(g))

    def relay(g):
        @pl.when(place >= 1)
        def _():
            received(own_next(g))

        @pl.when(after & (place >= 1))
        def _():
            start(pass_on(g))

        send(g + ahead)

    first = jnp.where(z == 1, KEY_VALUE_HEADS, jnp.where(last, 2, 1))
    pl.loop(0, first)(relay)

    for copy in tables:
        copy.wait()

    base = place * rows
    query_off = lax.broadcasted_iota(jnp.int32, (1, rows), 1)
    query_pos = query_off + base

    def doc_step(n, carry):
        start, begin = carry
        begin = jnp.where(query_pos >= start, start, begin)
        return start + doc_ref[n], begin

    _, begin = lax.fori_loop(
        0, doc_ref.shape[0], doc_step, (jnp.int32(0), jnp.zeros((1, rows), jnp.int32))
    )
    begin_rel = begin - base + edge

    scale = 1.0 / math.sqrt(HEAD_SIZE)
    scale2 = scale * math.log2(math.e)
    key_off = lax.broadcasted_iota(jnp.int32, (rows, PAIR * rows), 0)
    causal = key_off <= jnp.concatenate([query_off] * PAIR, axis=1)
    own_or_far = jnp.where(causal, key_off + edge, key_off)
    own_part = jnp.where(causal, 1.0, 0.0).astype(jnp.bfloat16)

    def take(total_ref, source, g):
        backward(g, 0, source, -1).wait_recv()
        total_ref[:, cols(g)] = (
            total_ref[:, cols(g)].astype(jnp.float32) + in_buf[source, :, cols(g)].astype(jnp.float32)
        ).astype(total_ref.dtype)

    def turned_keys(g):
        return kx_ref[:, cols(g)].astype(jnp.float32).T.astype(jnp.bfloat16)

    def query_grads(g, keys_t, pair):
        lanes = slice(pair * PAIR * rows, (pair + 1) * PAIR * rows)
        dq_t = lax.dot_general(
            keys_t, ds_ref[:, lanes], (((1,), (0,)), ((), ())), preferred_element_type=jnp.float32
        )
        for n in range(PAIR):
            dq_ref[:, cols(g * group + pair * PAIR + n)] = (
                dq_t[:, n * rows : (n + 1) * rows].T.astype(jnp.bfloat16)
            )

    def straight(g):
        return g >= KEY_VALUE_HEADS - DIRECT

    def join(g):
        take(out_buf.at[1], 2, g)

        @pl.when(place >= 2)
        def _():
            backward(g, 1, 1, -2).start()

    @pl.loop(0, KEY_VALUE_HEADS)
    def _(g):
        for copy in keys_of(g) + rows_of(g):
            copy.wait()

        @pl.when(g + first < KEY_VALUE_HEADS)
        def _():
            relay(g + first)

        @pl.when(place >= 2)
        def _():
            received(pass_on(g))

        keys = kx_ref[:, cols(g)]
        values = vx_ref[:, cols(g)]
        before = lax.div(g * (KEY_VALUE_HEADS - 1), KEY_VALUE_HEADS)
        keys_t = turned_keys(before)
        for pair in range(group // PAIR):
            query_grads(before, keys_t, pair)
            heads = [g * group + pair * PAIR + n for n in range(PAIR)]
            queries = jnp.concatenate([q_ref[:, cols(h)] for h in heads], axis=0)
            gradout = jnp.concatenate([do_ref[:, cols(h)] for h in heads], axis=0)
            lowest = jnp.concatenate(
                [jnp.maximum(begin_rel, query_off + (edge + 1) - win_ref[h]) for h in heads],
                axis=1,
            )
            def against(block):
                far, near, own = (
                    lax.dot_general(
                        block[t * rows : (t + 1) * rows],
                        other,
                        (((1,), (1,)), ((), ())),
                        preferred_element_type=jnp.float32,
                    )
                    for t in range(HALO + 1)
                )
                return jnp.where(causal, own, far), near

            other = queries
            outer, inner = against(keys)
            outer = jnp.where(own_or_far >= lowest, outer, NEG_FILL)
            inner = jnp.where(key_off >= lowest - rows, inner, NEG_FILL)
            row_max = jnp.max(jnp.maximum(outer, inner), axis=0, keepdims=True)
            outer = jnp.exp2((outer - row_max) * scale2)
            inner = jnp.exp2((inner - row_max) * scale2)
            other = gradout
            outer_d, inner_d = against(values)
            inverse = 1.0 / jnp.sum(outer + inner, axis=0, keepdims=True)
            delta = jnp.sum(outer * outer_d + inner * inner_d, axis=0, keepdims=True) * inverse
            factor = inverse * scale
            outer = ((outer * factor) * (outer_d - delta)).astype(jnp.bfloat16)
            inner = ((inner * factor) * (inner_d - delta)).astype(jnp.bfloat16)
            own = outer * own_part
            lanes = slice(pair * PAIR * rows, (pair + 1) * PAIR * rows)
            ds_ref[:rows, lanes] = outer - own
            ds_ref[rows:edge, lanes] = inner
            ds_ref[edge:, lanes] = own
            qs_ref[pair * PAIR * rows : (pair + 1) * PAIR * rows, :] = queries

        dkx = lax.dot_general(
            ds_ref[...], qs_ref[...], (((1,), (0,)), ((), ())), preferred_element_type=jnp.float32
        )
        own_ref[:, cols(g)] = dkx[edge:]
        out_buf[0, :, cols(g)] = dkx[rows:edge].astype(jnp.bfloat16)
        out_buf[1, :, cols(g)] = dkx[:rows].astype(jnp.bfloat16)

        @pl.when(sends_on & jnp.logical_not(straight(g)))
        def _():
            backward(g, 0, 2, 1).start()

        @pl.when((straight(g) | jnp.logical_not(sends_on)) & (place >= 1))
        def _():
            backward(g, 0, 0, -1).start()

        @pl.when((straight(g) | jnp.logical_not(joins)) & (place >= 2))
        def _():
            backward(g, 1, 1, -2).start()

        @pl.when(joins & (g >= 1) & jnp.logical_not(straight(g - 1)))
        def _():
            join(g - 1)

    final_keys_t = turned_keys(KEY_VALUE_HEADS - 1)
    for pair in range(group // PAIR):
        query_grads(KEY_VALUE_HEADS - 1, final_keys_t, pair)

    @pl.when(joins & jnp.logical_not(straight(KEY_VALUE_HEADS - 1)))
    def _():
        join(KEY_VALUE_HEADS - 1)

    @pl.loop(0, KEY_VALUE_HEADS)
    def _(g):
        for there, copies in ((after, own_next), (after & (place >= 1), pass_on)):

            @pl.when(there)
            def _():
                sent(copies(g))

        @pl.when(place >= 1)
        def _():
            backward(g, 0, 0, -1).wait_send()

        @pl.when(place >= 2)
        def _():
            backward(g, 1, 1, -2).wait_send()

    @pl.loop(0, KEY_VALUE_HEADS)
    def _(g):
        @pl.when((z == 0) | (z == hs_count - 2) | (straight(g) & after))
        def _():
            take(own_ref, 0, g)

        @pl.when(place + 2 < total)
        def _():
            take(own_ref, 1, g)

        dk_ref[:, cols(g)] = own_ref[:, cols(g)].astype(jnp.bfloat16)


def store_kernel(dq_ref, dk_ref, dq_hbm, dk_hbm, sem):
    copies = (
        pltpu.make_async_copy(dq_ref, dq_hbm, sem.at[0]),
        pltpu.make_async_copy(dk_ref, dk_hbm, sem.at[1]),
    )
    for copy in copies:
        copy.start()
    for copy in copies:
        copy.wait()


def shards(queries, key_matrix, value_matrix, output_gradient, doc_lengths, windows):
    rows = queries.shape[0]
    ctx_count, hs_count = lax.axis_size("ctx"), lax.axis_size("hs")
    if HALO * rows < WINDOW_LIMIT or hs_count < 3:
        raise ValueError("unsupported shape")
    groups = KEY_VALUE_HEADS
    ext = (HALO + 1) * rows
    kv_cols = key_matrix.shape[1]
    any_spec = pl.BlockSpec(memory_space=pltpu.HBM)
    grads = pl.pallas_call(
        functools.partial(attention_kernel, ctx_count, hs_count, rows),
        out_shape=(
            pltpu.VMEM(queries.shape, jnp.bfloat16),
            pltpu.VMEM(key_matrix.shape, jnp.bfloat16),
        ),
        in_specs=[any_spec, any_spec, any_spec, any_spec, any_spec, any_spec],
        out_specs=(pl.BlockSpec(memory_space=pltpu.VMEM), pl.BlockSpec(memory_space=pltpu.VMEM)),
        scratch_shapes=[
            pltpu.SMEM(doc_lengths.shape, jnp.int32),
            pltpu.SMEM(windows.shape, jnp.int32),
            pltpu.VMEM(queries.shape, jnp.bfloat16),
            pltpu.VMEM(queries.shape, jnp.bfloat16),
            pltpu.VMEM((ext, kv_cols), jnp.bfloat16),
            pltpu.VMEM((ext, kv_cols), jnp.bfloat16),
            pltpu.VMEM((rows, kv_cols), jnp.float32),
            pltpu.VMEM((ext, QUERY_HEADS // KEY_VALUE_HEADS * rows), jnp.bfloat16),
            pltpu.VMEM((QUERY_HEADS // KEY_VALUE_HEADS * rows, HEAD_SIZE), jnp.bfloat16),
            pltpu.VMEM((2, rows, kv_cols), jnp.bfloat16),
            pltpu.VMEM((3, rows, kv_cols), jnp.bfloat16),
            pltpu.SemaphoreType.DMA((2,)),
            pltpu.SemaphoreType.DMA((4, groups)),
            pltpu.SemaphoreType.DMA((2, 2, groups)),
            pltpu.SemaphoreType.DMA((2, HALO, groups)),
            pltpu.SemaphoreType.DMA((2, groups)),
            pltpu.SemaphoreType.DMA((3, groups)),
        ],
        compiler_params=pltpu.CompilerParams(collective_id=0, has_side_effects=True),
    )(doc_lengths, windows, queries, key_matrix, value_matrix, output_gradient)
    vmem_spec = pl.BlockSpec(memory_space=pltpu.VMEM)
    return pl.pallas_call(
        store_kernel,
        out_shape=(
            jax.ShapeDtypeStruct(queries.shape, jnp.bfloat16),
            jax.ShapeDtypeStruct(key_matrix.shape, jnp.bfloat16),
        ),
        in_specs=[pl.BlockSpec(memory_space=pl.ANY)] * 2,
        out_specs=(any_spec, any_spec),
        scratch_shapes=[pltpu.SemaphoreType.DMA((2,))],
        compiler_params=pltpu.CompilerParams(vmem_limit_bytes=2**20),
    )(*grads)


def solution(mesh):
    spec = P(("ctx", "hs"), None)
    return jax.shard_map(
        shards,
        mesh=mesh,
        in_specs=(spec, spec, spec, spec, P(), P()),
        out_specs=(spec, spec),
        check_vma=False,
    )
```

```python
import functools
import math

import jax
import jax.numpy as jnp
from jax import lax
from jax.experimental import pallas as pl
from jax.experimental.pallas import tpu as pltpu
from jax.sharding import PartitionSpec as P

QUERY_HEADS = 32
KEY_VALUE_HEADS = 4
HEAD_SIZE = 128
WINDOW_LIMIT = 256

NEG_FILL = -1e30
MESH = pl.DeviceIdType.MESH
PAIR = 2
HALO = 2
AHEAD = 2
DIRECT = 1


def attention_kernel(
    ctx_count,
    hs_count,
    rows,
    doc_hbm,
    win_hbm,
    q_hbm,
    k_hbm,
    v_hbm,
    do_hbm,
    dq_ref,
    dk_ref,
    doc_ref,
    win_ref,
    q_ref,
    do_ref,
    kx_ref,
    vx_ref,
    own_ref,
    ds_ref,
    qs_ref,
    out_buf,
    in_buf,
    table_sem,
    local_sem,
    fs_sem,
    fr_sem,
    bs_sem,
    br_sem,
):
    group = QUERY_HEADS // KEY_VALUE_HEADS
    group_cols = group * HEAD_SIZE
    c, z = lax.axis_index("ctx"), lax.axis_index("hs")
    place = c * hs_count + z
    total = ctx_count * hs_count
    edge = HALO * rows
    ext = edge + rows

    after = place + 1 < total
    last = z == hs_count - 1
    sends_on = ((z >= 2) & (z <= hs_count - 2)) | ((z == 0) & (c > 0))
    joins = (z >= 3) | ((z == 1) & (c > 0))

    def at(step):
        index = place + step
        return (lax.div(index, hs_count), lax.rem(index, hs_count))

    def cols(g):
        return pl.ds(pl.multiple_of(g * HEAD_SIZE, HEAD_SIZE), HEAD_SIZE)

    def wide(g):
        return pl.ds(pl.multiple_of(g * group_cols, group_cols), group_cols)

    def rows_of(g):
        return (
            pltpu.make_async_copy(q_hbm.at[:, wide(g)], q_ref.at[:, wide(g)], local_sem.at[0, g]),
            pltpu.make_async_copy(
                do_hbm.at[:, wide(g)], do_ref.at[:, wide(g)], local_sem.at[1, g]
            ),
        )

    def keys_of(g):
        return (
            pltpu.make_async_copy(
                k_hbm.at[:, cols(g)], kx_ref.at[pl.ds(edge, rows), cols(g)], local_sem.at[2, g]
            ),
            pltpu.make_async_copy(
                v_hbm.at[:, cols(g)], vx_ref.at[pl.ds(edge, rows), cols(g)], local_sem.at[3, g]
            ),
        )

    def block_rows(slot):
        return pl.ds(edge - slot * rows, rows)

    def forward(kind, g, source, slot):
        pairs = ((k_hbm, kx_ref), (v_hbm, vx_ref))
        return tuple(
            pltpu.make_async_remote_copy(
                src_ref=src.at[:, cols(g)] if source == 0 else dst.at[block_rows(source), cols(g)],
                dst_ref=dst.at[block_rows(slot), cols(g)],
                send_sem=fs_sem.at[i, kind, g],
                recv_sem=fr_sem.at[i, slot - 1, g],
                device_id=at(1),
                device_id_type=MESH,
            )
            for i, (src, dst) in enumerate(pairs)
        )

    own_next = lambda g: forward(0, g, 0, 1)
    pass_on = lambda g: forward(1, g, 1, 2)

    def backward(g, part, target, step):
        return pltpu.make_async_remote_copy(
            src_ref=out_buf.at[part, :, cols(g)],
            dst_ref=in_buf.at[target, :, cols(g)],
            send_sem=bs_sem.at[part, g],
            recv_sem=br_sem.at[target, g],
            device_id=at(step),
            device_id_type=MESH,
        )

    def start(copies):
        for copy in copies:
            copy.start()

    def received(copies):
        for copy in copies:
            copy.wait_recv()

    def sent(copies):
        for copy in copies:
            copy.wait_send()

    barrier = pltpu.get_barrier_semaphore()

    @pl.when(place >= 1)
    def _():
        pl.semaphore_signal(barrier, inc=1, device_id=at(-1), device_id_type=MESH)

    tables = (
        pltpu.make_async_copy(doc_hbm, doc_ref, table_sem.at[0]),
        pltpu.make_async_copy(win_hbm, win_ref, table_sem.at[1]),
    )

    for slot in range(1, HALO + 1):

        @pl.when(place < slot)
        def _():
            kx_ref[block_rows(slot), :] = jnp.zeros((rows, kx_ref.shape[1]), kx_ref.dtype)
            vx_ref[block_rows(slot), :] = jnp.zeros((rows, vx_ref.shape[1]), vx_ref.dtype)

    @pl.when(after)
    def _():
        pl.semaphore_wait(barrier, 1)

    def send(g):
        @pl.when(after & (g < KEY_VALUE_HEADS))
        def _():
            start(own_next(g))

    ahead = jnp.where((z == 0) | (z == hs_count - 2), KEY_VALUE_HEADS, AHEAD)
    pl.loop(0, ahead)(send)
    start(tables)

    @pl.loop(0, KEY_VALUE_HEADS)
    def _(g):
        start(keys_of(g) + rows_of(g))

    def relay(g):
        @pl.when(place >= 1)
        def _():
            received(own_next(g))

        @pl.when(after & (place >= 1))
        def _():
            start(pass_on(g))

        send(g + ahead)

    first = jnp.where(z == 0, 2, jnp.where((z == 1) | last, KEY_VALUE_HEADS, 1))
    pl.loop(0, first)(relay)

    for copy in tables:
        copy.wait()

    base = place * rows
    query_off = lax.broadcasted_iota(jnp.int32, (1, rows), 1)
    query_pos = query_off + base

    def doc_step(n, carry):
        start, begin = carry
        begin = jnp.where(query_pos >= start, start, begin)
        return start + doc_ref[n], begin

    _, begin = lax.fori_loop(
        0, doc_ref.shape[0], doc_step, (jnp.int32(0), jnp.zeros((1, rows), jnp.int32))
    )
    begin_rel = begin - base + edge

    scale = 1.0 / math.sqrt(HEAD_SIZE)
    scale2 = scale * math.log2(math.e)
    key_off = lax.broadcasted_iota(jnp.int32, (rows, PAIR * rows), 0)
    causal = key_off <= jnp.concatenate([query_off] * PAIR, axis=1)
    own_or_far = jnp.where(causal, key_off + edge, key_off)
    own_part = jnp.where(causal, 1.0, 0.0).astype(jnp.bfloat16)

    def take(total_ref, source, g):
        backward(g, 0, source, -1).wait_recv()
        total_ref[:, cols(g)] = (
            total_ref[:, cols(g)].astype(jnp.float32) + in_buf[source, :, cols(g)].astype(jnp.float32)
        ).astype(total_ref.dtype)

    def turned_keys(g):
        return kx_ref[:, cols(g)].astype(jnp.float32).T.astype(jnp.bfloat16)

    def query_grads(g, keys_t, pair):
        lanes = slice(pair * PAIR * rows, (pair + 1) * PAIR * rows)
        dq_t = lax.dot_general(
            keys_t, ds_ref[:, lanes], (((1,), (0,)), ((), ())), preferred_element_type=jnp.float32
        )
        for n in range(PAIR):
            dq_ref[:, cols(g * group + pair * PAIR + n)] = (
                dq_t[:, n * rows : (n + 1) * rows].T.astype(jnp.bfloat16)
            )

    def straight(g):
        return g >= KEY_VALUE_HEADS - DIRECT

    def join(g):
        take(out_buf.at[1], 2, g)

        @pl.when(place >= 2)
        def _():
            backward(g, 1, 1, -2).start()

    @pl.loop(0, KEY_VALUE_HEADS)
    def _(g):
        for copy in keys_of(g) + rows_of(g):
            copy.wait()

        @pl.when(g + first < KEY_VALUE_HEADS)
        def _():
            relay(g + first)

        @pl.when(place >= 2)
        def _():
            received(pass_on(g))

        keys = kx_ref[:, cols(g)]
        values = vx_ref[:, cols(g)]
        before = lax.div(g * (KEY_VALUE_HEADS - 1), KEY_VALUE_HEADS)
        keys_t = turned_keys(before)
        for pair in range(group // PAIR):
            query_grads(before, keys_t, pair)
            heads = [g * group + pair * PAIR + n for n in range(PAIR)]
            queries = jnp.concatenate([q_ref[:, cols(h)] for h in heads], axis=0)
            gradout = jnp.concatenate([do_ref[:, cols(h)] for h in heads], axis=0)
            lowest = jnp.concatenate(
                [jnp.maximum(begin_rel, query_off + (edge + 1) - win_ref[h]) for h in heads],
                axis=1,
            )
            def against(block):
                far, near, own = (
                    lax.dot_general(
                        block[t * rows : (t + 1) * rows],
                        other,
                        (((1,), (1,)), ((), ())),
                        preferred_element_type=jnp.float32,
                    )
                    for t in range(HALO + 1)
                )
                return jnp.where(causal, own, far), near

            other = queries
            outer, inner = against(keys)
            outer = jnp.where(own_or_far >= lowest, outer, NEG_FILL)
            inner = jnp.where(key_off >= lowest - rows, inner, NEG_FILL)
            row_max = jnp.max(jnp.maximum(outer, inner), axis=0, keepdims=True)
            outer = jnp.exp2((outer - row_max) * scale2)
            inner = jnp.exp2((inner - row_max) * scale2)
            other = gradout
            outer_d, inner_d = against(values)
            inverse = 1.0 / jnp.sum(outer + inner, axis=0, keepdims=True)
            delta = jnp.sum(outer * outer_d + inner * inner_d, axis=0, keepdims=True) * inverse
            factor = inverse * scale
            outer = ((outer * factor) * (outer_d - delta)).astype(jnp.bfloat16)
            inner = ((inner * factor) * (inner_d - delta)).astype(jnp.bfloat16)
            own = outer * own_part
            lanes = slice(pair * PAIR * rows, (pair + 1) * PAIR * rows)
            ds_ref[:rows, lanes] = outer - own
            ds_ref[rows:edge, lanes] = inner
            ds_ref[edge:, lanes] = own
            qs_ref[pair * PAIR * rows : (pair + 1) * PAIR * rows, :] = queries

        dkx = lax.dot_general(
            ds_ref[...], qs_ref[...], (((1,), (0,)), ((), ())), preferred_element_type=jnp.float32
        )
        own_ref[:, cols(g)] = dkx[edge:]
        out_buf[0, :, cols(g)] = dkx[rows:edge].astype(jnp.bfloat16)
        out_buf[1, :, cols(g)] = dkx[:rows].astype(jnp.bfloat16)

        @pl.when(sends_on & jnp.logical_not(straight(g)))
        def _():
            backward(g, 0, 2, 1).start()

        @pl.when((straight(g) | jnp.logical_not(sends_on)) & (place >= 1))
        def _():
            backward(g, 0, 0, -1).start()

        @pl.when((straight(g) | jnp.logical_not(joins)) & (place >= 2))
        def _():
            backward(g, 1, 1, -2).start()

        @pl.when(joins & (g >= 1) & jnp.logical_not(straight(g - 1)))
        def _():
            join(g - 1)

    final_keys_t = turned_keys(KEY_VALUE_HEADS - 1)
    for pair in range(group // PAIR):
        query_grads(KEY_VALUE_HEADS - 1, final_keys_t, pair)

    @pl.when(joins & jnp.logical_not(straight(KEY_VALUE_HEADS - 1)))
    def _():
        join(KEY_VALUE_HEADS - 1)

    @pl.loop(0, KEY_VALUE_HEADS)
    def _(g):
        for there, copies in ((after, own_next), (after & (place >= 1), pass_on)):

            @pl.when(there)
            def _():
                sent(copies(g))

        @pl.when(place >= 1)
        def _():
            backward(g, 0, 0, -1).wait_send()

        @pl.when(place >= 2)
        def _():
            backward(g, 1, 1, -2).wait_send()

    @pl.loop(0, KEY_VALUE_HEADS)
    def _(g):
        @pl.when((z == 0) | (z == hs_count - 2) | (straight(g) & after))
        def _():
            take(own_ref, 0, g)

        @pl.when(place + 2 < total)
        def _():
            take(own_ref, 1, g)

        dk_ref[:, cols(g)] = own_ref[:, cols(g)].astype(jnp.bfloat16)


def store_kernel(dq_ref, dk_ref, dq_hbm, dk_hbm, sem):
    copies = (
        pltpu.make_async_copy(dq_ref, dq_hbm, sem.at[0]),
        pltpu.make_async_copy(dk_ref, dk_hbm, sem.at[1]),
    )
    for copy in copies:
        copy.start()
    for copy in copies:
        copy.wait()


def shards(queries, key_matrix, value_matrix, output_gradient, doc_lengths, windows):
    rows = queries.shape[0]
    ctx_count, hs_count = lax.axis_size("ctx"), lax.axis_size("hs")
    if HALO * rows < WINDOW_LIMIT or hs_count < 3:
        raise ValueError("unsupported shape")
    groups = KEY_VALUE_HEADS
    ext = (HALO + 1) * rows
    kv_cols = key_matrix.shape[1]
    any_spec = pl.BlockSpec(memory_space=pltpu.HBM)
    grads = pl.pallas_call(
        functools.partial(attention_kernel, ctx_count, hs_count, rows),
        out_shape=(
            pltpu.VMEM(queries.shape, jnp.bfloat16),
            pltpu.VMEM(key_matrix.shape, jnp.bfloat16),
        ),
        in_specs=[any_spec, any_spec, any_spec, any_spec, any_spec, any_spec],
        out_specs=(pl.BlockSpec(memory_space=pltpu.VMEM), pl.BlockSpec(memory_space=pltpu.VMEM)),
        scratch_shapes=[
            pltpu.SMEM(doc_lengths.shape, jnp.int32),
            pltpu.SMEM(windows.shape, jnp.int32),
            pltpu.VMEM(queries.shape, jnp.bfloat16),
            pltpu.VMEM(queries.shape, jnp.bfloat16),
            pltpu.VMEM((ext, kv_cols), jnp.bfloat16),
            pltpu.VMEM((ext, kv_cols), jnp.bfloat16),
            pltpu.VMEM((rows, kv_cols), jnp.float32),
            pltpu.VMEM((ext, QUERY_HEADS // KEY_VALUE_HEADS * rows), jnp.bfloat16),
            pltpu.VMEM((QUERY_HEADS // KEY_VALUE_HEADS * rows, HEAD_SIZE), jnp.bfloat16),
            pltpu.VMEM((2, rows, kv_cols), jnp.bfloat16),
            pltpu.VMEM((3, rows, kv_cols), jnp.bfloat16),
            pltpu.SemaphoreType.DMA((2,)),
            pltpu.SemaphoreType.DMA((4, groups)),
            pltpu.SemaphoreType.DMA((2, 2, groups)),
            pltpu.SemaphoreType.DMA((2, HALO, groups)),
            pltpu.SemaphoreType.DMA((2, groups)),
            pltpu.SemaphoreType.DMA((3, groups)),
        ],
        compiler_params=pltpu.CompilerParams(collective_id=0, has_side_effects=True),
    )(doc_lengths, windows, queries, key_matrix, value_matrix, output_gradient)
    vmem_spec = pl.BlockSpec(memory_space=pltpu.VMEM)
    return pl.pallas_call(
        store_kernel,
        out_shape=(
            jax.ShapeDtypeStruct(queries.shape, jnp.bfloat16),
            jax.ShapeDtypeStruct(key_matrix.shape, jnp.bfloat16),
        ),
        in_specs=[pl.BlockSpec(memory_space=pl.ANY)] * 2,
        out_specs=(any_spec, any_spec),
        scratch_shapes=[pltpu.SemaphoreType.DMA((2,))],
        compiler_params=pltpu.CompilerParams(vmem_limit_bytes=2**20),
    )(*grads)


def solution(mesh):
    spec = P(("ctx", "hs"), None)
    return jax.shard_map(
        shards,
        mesh=mesh,
        in_specs=(spec, spec, spec, spec, P(), P()),
        out_specs=(spec, spec),
        check_vma=False,
    )
```

```python
import functools
import math

import jax
import jax.numpy as jnp
from jax import lax
from jax.experimental import pallas as pl
from jax.experimental.pallas import tpu as pltpu
from jax.sharding import PartitionSpec as P

QUERY_HEADS = 32
KEY_VALUE_HEADS = 4
HEAD_SIZE = 128
WINDOW_LIMIT = 256

NEG_FILL = -1e30
MESH = pl.DeviceIdType.MESH
PAIR = 2
HALO = 2
AHEAD = 2
DIRECT = 1


def attention_kernel(
    ctx_count,
    hs_count,
    rows,
    doc_hbm,
    win_hbm,
    q_hbm,
    k_hbm,
    v_hbm,
    do_hbm,
    dq_ref,
    dk_ref,
    doc_ref,
    win_ref,
    q_ref,
    do_ref,
    kx_ref,
    vx_ref,
    own_ref,
    ds_ref,
    qs_ref,
    out_buf,
    in_buf,
    table_sem,
    local_sem,
    fs_sem,
    fr_sem,
    bs_sem,
    br_sem,
):
    group = QUERY_HEADS // KEY_VALUE_HEADS
    group_cols = group * HEAD_SIZE
    c, z = lax.axis_index("ctx"), lax.axis_index("hs")
    place = c * hs_count + z
    total = ctx_count * hs_count
    edge = HALO * rows
    ext = edge + rows

    after = place + 1 < total
    last = z == hs_count - 1
    sends_on = ((z >= 2) & (z <= hs_count - 2)) | ((z == 0) & (c > 0))
    joins = (z >= 3) | ((z == 1) & (c > 0))

    def at(step):
        index = place + step
        return (lax.div(index, hs_count), lax.rem(index, hs_count))

    def cols(g):
        return pl.ds(pl.multiple_of(g * HEAD_SIZE, HEAD_SIZE), HEAD_SIZE)

    def wide(g):
        return pl.ds(pl.multiple_of(g * group_cols, group_cols), group_cols)

    def rows_of(g):
        return (
            pltpu.make_async_copy(q_hbm.at[:, wide(g)], q_ref.at[:, wide(g)], local_sem.at[0, g]),
            pltpu.make_async_copy(
                do_hbm.at[:, wide(g)], do_ref.at[:, wide(g)], local_sem.at[1, g]
            ),
        )

    def keys_of(g):
        return (
            pltpu.make_async_copy(
                k_hbm.at[:, cols(g)], kx_ref.at[pl.ds(edge, rows), cols(g)], local_sem.at[2, g]
            ),
            pltpu.make_async_copy(
                v_hbm.at[:, cols(g)], vx_ref.at[pl.ds(edge, rows), cols(g)], local_sem.at[3, g]
            ),
        )

    def block_rows(slot):
        return pl.ds(edge - slot * rows, rows)

    def forward(kind, g, source, slot):
        pairs = ((k_hbm, kx_ref), (v_hbm, vx_ref))
        return tuple(
            pltpu.make_async_remote_copy(
                src_ref=src.at[:, cols(g)] if source == 0 else dst.at[block_rows(source), cols(g)],
                dst_ref=dst.at[block_rows(slot), cols(g)],
                send_sem=fs_sem.at[i, kind, g],
                recv_sem=fr_sem.at[i, slot - 1, g],
                device_id=at(1),
                device_id_type=MESH,
            )
            for i, (src, dst) in enumerate(pairs)
        )

    own_next = lambda g: forward(0, g, 0, 1)
    pass_on = lambda g: forward(1, g, 1, 2)

    def backward(g, part, target, step):
        return pltpu.make_async_remote_copy(
            src_ref=out_buf.at[part, :, cols(g)],
            dst_ref=in_buf.at[target, :, cols(g)],
            send_sem=bs_sem.at[part, g],
            recv_sem=br_sem.at[target, g],
            device_id=at(step),
            device_id_type=MESH,
        )

    def start(copies):
        for copy in copies:
            copy.start()

    def received(copies):
        for copy in copies:
            copy.wait_recv()

    def sent(copies):
        for copy in copies:
            copy.wait_send()

    barrier = pltpu.get_barrier_semaphore()

    @pl.when(place >= 1)
    def _():
        pl.semaphore_signal(barrier, inc=1, device_id=at(-1), device_id_type=MESH)

    tables = (
        pltpu.make_async_copy(doc_hbm, doc_ref, table_sem.at[0]),
        pltpu.make_async_copy(win_hbm, win_ref, table_sem.at[1]),
    )

    for slot in range(1, HALO + 1):

        @pl.when(place < slot)
        def _():
            kx_ref[block_rows(slot), :] = jnp.zeros((rows, kx_ref.shape[1]), kx_ref.dtype)
            vx_ref[block_rows(slot), :] = jnp.zeros((rows, vx_ref.shape[1]), vx_ref.dtype)

    @pl.when(after)
    def _():
        pl.semaphore_wait(barrier, 1)

    def send(g):
        @pl.when(after & (g < KEY_VALUE_HEADS))
        def _():
            start(own_next(g))

    ahead = jnp.where((z == 0) | (z == hs_count - 2), KEY_VALUE_HEADS, AHEAD)
    pl.loop(0, ahead)(send)
    start(tables)

    @pl.loop(0, KEY_VALUE_HEADS)
    def _(g):
        start(keys_of(g) + rows_of(g))

    def relay(g):
        @pl.when(place >= 1)
        def _():
            received(own_next(g))

        @pl.when(after & (place >= 1))
        def _():
            start(pass_on(g))

        send(g + ahead)

    first = jnp.where(z == 0, 2, jnp.where((z == 1) | last, KEY_VALUE_HEADS, 1))
    pl.loop(0, first)(relay)

    for copy in tables:
        copy.wait()

    base = place * rows
    query_off = lax.broadcasted_iota(jnp.int32, (1, rows), 1)
    query_pos = query_off + base

    def doc_step(n, carry):
        start, begin = carry
        begin = jnp.where(query_pos >= start, start, begin)
        return start + doc_ref[n], begin

    _, begin = lax.fori_loop(
        0, doc_ref.shape[0], doc_step, (jnp.int32(0), jnp.zeros((1, rows), jnp.int32))
    )
    begin_rel = begin - base + edge

    scale = 1.0 / math.sqrt(HEAD_SIZE)
    scale2 = scale * math.log2(math.e)
    key_off = lax.broadcasted_iota(jnp.int32, (rows, PAIR * rows), 0)
    causal = key_off <= jnp.concatenate([query_off] * PAIR, axis=1)
    own_or_far = jnp.where(causal, key_off + edge, key_off)
    own_part = jnp.where(causal, 1.0, 0.0).astype(jnp.bfloat16)

    def take(total_ref, source, g):
        backward(g, 0, source, -1).wait_recv()
        total_ref[:, cols(g)] = (
            total_ref[:, cols(g)].astype(jnp.float32) + in_buf[source, :, cols(g)].astype(jnp.float32)
        ).astype(total_ref.dtype)

    def turned_keys(g):
        return kx_ref[:, cols(g)].astype(jnp.float32).T.astype(jnp.bfloat16)

    def query_grads(g, keys_t, pair):
        lanes = slice(pair * PAIR * rows, (pair + 1) * PAIR * rows)
        dq_t = lax.dot_general(
            keys_t, ds_ref[:, lanes], (((1,), (0,)), ((), ())), preferred_element_type=jnp.float32
        )
        for n in range(PAIR):
            dq_ref[:, cols(g * group + pair * PAIR + n)] = (
                dq_t[:, n * rows : (n + 1) * rows].T.astype(jnp.bfloat16)
            )

    def straight(g):
        return g >= KEY_VALUE_HEADS - DIRECT

    def join(g):
        take(out_buf.at[1], 2, g)

        @pl.when(place >= 2)
        def _():
            backward(g, 1, 1, -2).start()

    @pl.loop(0, KEY_VALUE_HEADS)
    def _(g):
        for copy in keys_of(g) + rows_of(g):
            copy.wait()

        @pl.when(g + first < KEY_VALUE_HEADS)
        def _():
            relay(g + first)

        @pl.when(place >= 2)
        def _():
            received(pass_on(g))

        keys = kx_ref[:, cols(g)]
        values = vx_ref[:, cols(g)]
        before = lax.div(g * (KEY_VALUE_HEADS - 1), KEY_VALUE_HEADS)
        keys_t = turned_keys(before)
        for pair in range(group // PAIR):
            query_grads(before, keys_t, pair)
            heads = [g * group + pair * PAIR + n for n in range(PAIR)]
            queries = jnp.concatenate([q_ref[:, cols(h)] for h in heads], axis=0)
            gradout = jnp.concatenate([do_ref[:, cols(h)] for h in heads], axis=0)
            lowest = jnp.concatenate(
                [jnp.maximum(begin_rel, query_off + (edge + 1) - win_ref[h]) for h in heads],
                axis=1,
            )
            def against(block):
                far, near, own = (
                    lax.dot_general(
                        block[t * rows : (t + 1) * rows],
                        other,
                        (((1,), (1,)), ((), ())),
                        preferred_element_type=jnp.float32,
                    )
                    for t in range(HALO + 1)
                )
                return jnp.where(causal, own, far), near

            other = queries
            outer, inner = against(keys)
            outer = jnp.where(own_or_far >= lowest, outer, NEG_FILL)
            inner = jnp.where(key_off >= lowest - rows, inner, NEG_FILL)
            row_max = jnp.max(jnp.maximum(outer, inner), axis=0, keepdims=True)
            outer = jnp.exp2((outer - row_max) * scale2)
            inner = jnp.exp2((inner - row_max) * scale2)
            other = gradout
            outer_d, inner_d = against(values)
            inverse = 1.0 / jnp.sum(outer + inner, axis=0, keepdims=True)
            delta = jnp.sum(outer * outer_d + inner * inner_d, axis=0, keepdims=True) * inverse
            factor = inverse * scale
            outer = ((outer * factor) * (outer_d - delta)).astype(jnp.bfloat16)
            inner = ((inner * factor) * (inner_d - delta)).astype(jnp.bfloat16)
            own = outer * own_part
            lanes = slice(pair * PAIR * rows, (pair + 1) * PAIR * rows)
            ds_ref[:rows, lanes] = outer - own
            ds_ref[rows:edge, lanes] = inner
            ds_ref[edge:, lanes] = own
            qs_ref[pair * PAIR * rows : (pair + 1) * PAIR * rows, :] = queries

        dkx = lax.dot_general(
            ds_ref[...], qs_ref[...], (((1,), (0,)), ((), ())), preferred_element_type=jnp.float32
        )
        own_ref[:, cols(g)] = dkx[edge:]
        out_buf[0, :, cols(g)] = dkx[rows:edge].astype(jnp.bfloat16)
        out_buf[1, :, cols(g)] = dkx[:rows].astype(jnp.bfloat16)

        @pl.when(sends_on & jnp.logical_not(straight(g)))
        def _():
            backward(g, 0, 2, 1).start()

        @pl.when((straight(g) | jnp.logical_not(sends_on)) & (place >= 1))
        def _():
            backward(g, 0, 0, -1).start()

        @pl.when((straight(g) | jnp.logical_not(joins)) & (place >= 2))
        def _():
            backward(g, 1, 1, -2).start()

        @pl.when(joins & (g >= 1) & jnp.logical_not(straight(g - 1)))
        def _():
            join(g - 1)

    final_keys_t = turned_keys(KEY_VALUE_HEADS - 1)
    for pair in range(group // PAIR):
        query_grads(KEY_VALUE_HEADS - 1, final_keys_t, pair)

    @pl.when(joins & jnp.logical_not(straight(KEY_VALUE_HEADS - 1)))
    def _():
        join(KEY_VALUE_HEADS - 1)

    @pl.loop(0, KEY_VALUE_HEADS)
    def _(g):
        for there, copies in ((after, own_next), (after & (place >= 1), pass_on)):

            @pl.when(there)
            def _():
                sent(copies(g))

        @pl.when(place >= 1)
        def _():
            backward(g, 0, 0, -1).wait_send()

        @pl.when(place >= 2)
        def _():
            backward(g, 1, 1, -2).wait_send()

    @pl.loop(0, KEY_VALUE_HEADS)
    def _(g):
        from_next = (z == 0) | (z == hs_count - 2) | (straight(g) & after)
        total_grad = own_ref[:, cols(g)]
        for source, there in ((0, from_next), (1, place + 2 < total)):

            @pl.when(there)
            def _():
                backward(g, 0, source, -1).wait_recv()

        for source, there in ((0, from_next), (1, place + 2 < total)):
            part = in_buf[source, :, cols(g)].astype(jnp.float32)
            total_grad = total_grad + jnp.where(there, part, 0.0)
        dk_ref[:, cols(g)] = total_grad.astype(jnp.bfloat16)


def store_kernel(dq_ref, dk_ref, dq_hbm, dk_hbm, sem):
    copies = (
        pltpu.make_async_copy(dq_ref, dq_hbm, sem.at[0]),
        pltpu.make_async_copy(dk_ref, dk_hbm, sem.at[1]),
    )
    for copy in copies:
        copy.start()
    for copy in copies:
        copy.wait()


def shards(queries, key_matrix, value_matrix, output_gradient, doc_lengths, windows):
    rows = queries.shape[0]
    ctx_count, hs_count = lax.axis_size("ctx"), lax.axis_size("hs")
    if HALO * rows < WINDOW_LIMIT or hs_count < 3:
        raise ValueError("unsupported shape")
    groups = KEY_VALUE_HEADS
    ext = (HALO + 1) * rows
    kv_cols = key_matrix.shape[1]
    any_spec = pl.BlockSpec(memory_space=pltpu.HBM)
    grads = pl.pallas_call(
        functools.partial(attention_kernel, ctx_count, hs_count, rows),
        out_shape=(
            pltpu.VMEM(queries.shape, jnp.bfloat16),
            pltpu.VMEM(key_matrix.shape, jnp.bfloat16),
        ),
        in_specs=[any_spec, any_spec, any_spec, any_spec, any_spec, any_spec],
        out_specs=(pl.BlockSpec(memory_space=pltpu.VMEM), pl.BlockSpec(memory_space=pltpu.VMEM)),
        scratch_shapes=[
            pltpu.SMEM(doc_lengths.shape, jnp.int32),
            pltpu.SMEM(windows.shape, jnp.int32),
            pltpu.VMEM(queries.shape, jnp.bfloat16),
            pltpu.VMEM(queries.shape, jnp.bfloat16),
            pltpu.VMEM((ext, kv_cols), jnp.bfloat16),
            pltpu.VMEM((ext, kv_cols), jnp.bfloat16),
            pltpu.VMEM((rows, kv_cols), jnp.float32),
            pltpu.VMEM((ext, QUERY_HEADS // KEY_VALUE_HEADS * rows), jnp.bfloat16),
            pltpu.VMEM((QUERY_HEADS // KEY_VALUE_HEADS * rows, HEAD_SIZE), jnp.bfloat16),
            pltpu.VMEM((2, rows, kv_cols), jnp.bfloat16),
            pltpu.VMEM((3, rows, kv_cols), jnp.bfloat16),
            pltpu.SemaphoreType.DMA((2,)),
            pltpu.SemaphoreType.DMA((4, groups)),
            pltpu.SemaphoreType.DMA((2, 2, groups)),
            pltpu.SemaphoreType.DMA((2, HALO, groups)),
            pltpu.SemaphoreType.DMA((2, groups)),
            pltpu.SemaphoreType.DMA((3, groups)),
        ],
        compiler_params=pltpu.CompilerParams(collective_id=0, has_side_effects=True),
    )(doc_lengths, windows, queries, key_matrix, value_matrix, output_gradient)
    vmem_spec = pl.BlockSpec(memory_space=pltpu.VMEM)
    return pl.pallas_call(
        store_kernel,
        out_shape=(
            jax.ShapeDtypeStruct(queries.shape, jnp.bfloat16),
            jax.ShapeDtypeStruct(key_matrix.shape, jnp.bfloat16),
        ),
        in_specs=[pl.BlockSpec(memory_space=pl.ANY)] * 2,
        out_specs=(any_spec, any_spec),
        scratch_shapes=[pltpu.SemaphoreType.DMA((2,))],
        compiler_params=pltpu.CompilerParams(vmem_limit_bytes=2**20),
    )(*grads)


def solution(mesh):
    spec = P(("ctx", "hs"), None)
    return jax.shard_map(
        shards,
        mesh=mesh,
        in_specs=(spec, spec, spec, spec, P(), P()),
        out_specs=(spec, spec),
        check_vma=False,
    )
```

```python
import functools
import math

import jax
import jax.numpy as jnp
from jax import lax
from jax.experimental import pallas as pl
from jax.experimental.pallas import tpu as pltpu
from jax.sharding import PartitionSpec as P

QUERY_HEADS = 32
KEY_VALUE_HEADS = 4
HEAD_SIZE = 128
WINDOW_LIMIT = 256

NEG_FILL = -1e30
MESH = pl.DeviceIdType.MESH
PAIR = 2
HALO = 2
AHEAD = 2
DIRECT = 1


def attention_kernel(
    ctx_count,
    hs_count,
    rows,
    doc_hbm,
    win_hbm,
    q_hbm,
    k_hbm,
    v_hbm,
    do_hbm,
    dq_ref,
    dk_ref,
    doc_ref,
    win_ref,
    q_ref,
    do_ref,
    kx_ref,
    vx_ref,
    own_ref,
    ds_ref,
    qs_ref,
    out_buf,
    in_buf,
    table_sem,
    local_sem,
    fs_sem,
    fr_sem,
    bs_sem,
    br_sem,
):
    group = QUERY_HEADS // KEY_VALUE_HEADS
    group_cols = group * HEAD_SIZE
    c, z = lax.axis_index("ctx"), lax.axis_index("hs")
    place = c * hs_count + z
    total = ctx_count * hs_count
    edge = HALO * rows
    ext = edge + rows

    after = place + 1 < total
    last = z == hs_count - 1
    sends_on = ((z >= 2) & (z <= hs_count - 2)) | ((z == 0) & (c > 0))
    joins = (z >= 3) | ((z == 1) & (c > 0))

    def at(step):
        index = place + step
        return (lax.div(index, hs_count), lax.rem(index, hs_count))

    def cols(g):
        return pl.ds(pl.multiple_of(g * HEAD_SIZE, HEAD_SIZE), HEAD_SIZE)

    def wide(g):
        return pl.ds(pl.multiple_of(g * group_cols, group_cols), group_cols)

    def rows_of(g):
        return (
            pltpu.make_async_copy(q_hbm.at[:, wide(g)], q_ref.at[:, wide(g)], local_sem.at[0, g]),
            pltpu.make_async_copy(
                do_hbm.at[:, wide(g)], do_ref.at[:, wide(g)], local_sem.at[1, g]
            ),
        )

    def keys_of(g):
        return (
            pltpu.make_async_copy(
                k_hbm.at[:, cols(g)], kx_ref.at[pl.ds(edge, rows), cols(g)], local_sem.at[2, g]
            ),
            pltpu.make_async_copy(
                v_hbm.at[:, cols(g)], vx_ref.at[pl.ds(edge, rows), cols(g)], local_sem.at[3, g]
            ),
        )

    def block_rows(slot):
        return pl.ds(edge - slot * rows, rows)

    def forward(kind, g, source, slot):
        pairs = ((k_hbm, kx_ref), (v_hbm, vx_ref))
        return tuple(
            pltpu.make_async_remote_copy(
                src_ref=src.at[:, cols(g)] if source == 0 else dst.at[block_rows(source), cols(g)],
                dst_ref=dst.at[block_rows(slot), cols(g)],
                send_sem=fs_sem.at[i, kind, g],
                recv_sem=fr_sem.at[i, slot - 1, g],
                device_id=at(1),
                device_id_type=MESH,
            )
            for i, (src, dst) in enumerate(pairs)
        )

    own_next = lambda g: forward(0, g, 0, 1)
    pass_on = lambda g: forward(1, g, 1, 2)

    def backward(g, part, target, step):
        return pltpu.make_async_remote_copy(
            src_ref=out_buf.at[part, :, cols(g)],
            dst_ref=in_buf.at[target, :, cols(g)],
            send_sem=bs_sem.at[part, g],
            recv_sem=br_sem.at[target, g],
            device_id=at(step),
            device_id_type=MESH,
        )

    def start(copies):
        for copy in copies:
            copy.start()

    def received(copies):
        for copy in copies:
            copy.wait_recv()

    def sent(copies):
        for copy in copies:
            copy.wait_send()

    barrier = pltpu.get_barrier_semaphore()

    @pl.when(place >= 1)
    def _():
        pl.semaphore_signal(barrier, inc=1, device_id=at(-1), device_id_type=MESH)

    tables = (
        pltpu.make_async_copy(doc_hbm, doc_ref, table_sem.at[0]),
        pltpu.make_async_copy(win_hbm, win_ref, table_sem.at[1]),
    )

    for slot in range(1, HALO + 1):

        @pl.when(place < slot)
        def _():
            kx_ref[block_rows(slot), :] = jnp.zeros((rows, kx_ref.shape[1]), kx_ref.dtype)
            vx_ref[block_rows(slot), :] = jnp.zeros((rows, vx_ref.shape[1]), vx_ref.dtype)

    @pl.when(after)
    def _():
        pl.semaphore_wait(barrier, 1)

    def send(g):
        @pl.when(after & (g < KEY_VALUE_HEADS))
        def _():
            start(own_next(g))

    ahead = jnp.where((z == 0) | (z == hs_count - 2), KEY_VALUE_HEADS, AHEAD)
    pl.loop(0, ahead)(send)
    start(tables)

    @pl.loop(0, KEY_VALUE_HEADS)
    def _(g):
        start(keys_of(g) + rows_of(g))

    def relay(g):
        @pl.when(place >= 1)
        def _():
            received(own_next(g))

        @pl.when(after & (place >= 1))
        def _():
            start(pass_on(g))

        send(g + ahead)

    first = jnp.where(z == 0, 2, jnp.where((z == 1) | last, KEY_VALUE_HEADS, 2))
    pl.loop(0, first)(relay)

    for copy in tables:
        copy.wait()

    base = place * rows
    query_off = lax.broadcasted_iota(jnp.int32, (1, rows), 1)
    query_pos = query_off + base

    def doc_step(n, carry):
        start, begin = carry
        begin = jnp.where(query_pos >= start, start, begin)
        return start + doc_ref[n], begin

    _, begin = lax.fori_loop(
        0, doc_ref.shape[0], doc_step, (jnp.int32(0), jnp.zeros((1, rows), jnp.int32))
    )
    begin_rel = begin - base + edge

    scale = 1.0 / math.sqrt(HEAD_SIZE)
    scale2 = scale * math.log2(math.e)
    key_off = lax.broadcasted_iota(jnp.int32, (rows, PAIR * rows), 0)
    causal = key_off <= jnp.concatenate([query_off] * PAIR, axis=1)
    own_or_far = jnp.where(causal, key_off + edge, key_off)
    own_part = jnp.where(causal, 1.0, 0.0).astype(jnp.bfloat16)

    def take(total_ref, source, g):
        backward(g, 0, source, -1).wait_recv()
        total_ref[:, cols(g)] = (
            total_ref[:, cols(g)].astype(jnp.float32) + in_buf[source, :, cols(g)].astype(jnp.float32)
        ).astype(total_ref.dtype)

    def turned_keys(g):
        return kx_ref[:, cols(g)].astype(jnp.float32).T.astype(jnp.bfloat16)

    def query_grads(g, keys_t, pair):
        lanes = slice(pair * PAIR * rows, (pair + 1) * PAIR * rows)
        dq_t = lax.dot_general(
            keys_t, ds_ref[:, lanes], (((1,), (0,)), ((), ())), preferred_element_type=jnp.float32
        )
        for n in range(PAIR):
            dq_ref[:, cols(g * group + pair * PAIR + n)] = (
                dq_t[:, n * rows : (n + 1) * rows].T.astype(jnp.bfloat16)
            )

    def straight(g):
        return g >= KEY_VALUE_HEADS - DIRECT

    def join(g):
        take(out_buf.at[1], 2, g)

        @pl.when(place >= 2)
        def _():
            backward(g, 1, 1, -2).start()

    @pl.loop(0, KEY_VALUE_HEADS)
    def _(g):
        for copy in keys_of(g) + rows_of(g):
            copy.wait()

        @pl.when(g + first < KEY_VALUE_HEADS)
        def _():
            relay(g + first)

        @pl.when(place >= 2)
        def _():
            received(pass_on(g))

        keys = kx_ref[:, cols(g)]
        values = vx_ref[:, cols(g)]
        before = lax.div(g * (KEY_VALUE_HEADS - 1), KEY_VALUE_HEADS)
        keys_t = turned_keys(before)
        for pair in range(group // PAIR):
            query_grads(before, keys_t, pair)
            heads = [g * group + pair * PAIR + n for n in range(PAIR)]
            queries = jnp.concatenate([q_ref[:, cols(h)] for h in heads], axis=0)
            gradout = jnp.concatenate([do_ref[:, cols(h)] for h in heads], axis=0)
            lowest = jnp.concatenate(
                [jnp.maximum(begin_rel, query_off + (edge + 1) - win_ref[h]) for h in heads],
                axis=1,
            )
            def against(block):
                far, near, own = (
                    lax.dot_general(
                        block[t * rows : (t + 1) * rows],
                        other,
                        (((1,), (1,)), ((), ())),
                        preferred_element_type=jnp.float32,
                    )
                    for t in range(HALO + 1)
                )
                return jnp.where(causal, own, far), near

            other = queries
            outer, inner = against(keys)
            outer = jnp.where(own_or_far >= lowest, outer, NEG_FILL)
            inner = jnp.where(key_off >= lowest - rows, inner, NEG_FILL)
            row_max = jnp.max(jnp.maximum(outer, inner), axis=0, keepdims=True)
            outer = jnp.exp2((outer - row_max) * scale2)
            inner = jnp.exp2((inner - row_max) * scale2)
            other = gradout
            outer_d, inner_d = against(values)
            inverse = 1.0 / jnp.sum(outer + inner, axis=0, keepdims=True)
            delta = jnp.sum(outer * outer_d + inner * inner_d, axis=0, keepdims=True) * inverse
            factor = inverse * scale
            outer = ((outer * factor) * (outer_d - delta)).astype(jnp.bfloat16)
            inner = ((inner * factor) * (inner_d - delta)).astype(jnp.bfloat16)
            own = outer * own_part
            lanes = slice(pair * PAIR * rows, (pair + 1) * PAIR * rows)
            ds_ref[:rows, lanes] = outer - own
            ds_ref[rows:edge, lanes] = inner
            ds_ref[edge:, lanes] = own
            qs_ref[pair * PAIR * rows : (pair + 1) * PAIR * rows, :] = queries

        dkx = lax.dot_general(
            ds_ref[...], qs_ref[...], (((1,), (0,)), ((), ())), preferred_element_type=jnp.float32
        )
        own_ref[:, cols(g)] = dkx[edge:]
        out_buf[0, :, cols(g)] = dkx[rows:edge].astype(jnp.bfloat16)
        out_buf[1, :, cols(g)] = dkx[:rows].astype(jnp.bfloat16)

        @pl.when(sends_on & jnp.logical_not(straight(g)))
        def _():
            backward(g, 0, 2, 1).start()

        @pl.when((straight(g) | jnp.logical_not(sends_on)) & (place >= 1))
        def _():
            backward(g, 0, 0, -1).start()

        @pl.when((straight(g) | jnp.logical_not(joins)) & (place >= 2))
        def _():
            backward(g, 1, 1, -2).start()

        @pl.when(joins & (g >= 1) & jnp.logical_not(straight(g - 1)))
        def _():
            join(g - 1)

    final_keys_t = turned_keys(KEY_VALUE_HEADS - 1)
    for pair in range(group // PAIR):
        query_grads(KEY_VALUE_HEADS - 1, final_keys_t, pair)

    @pl.when(joins & jnp.logical_not(straight(KEY_VALUE_HEADS - 1)))
    def _():
        join(KEY_VALUE_HEADS - 1)

    @pl.loop(0, KEY_VALUE_HEADS)
    def _(g):
        for there, copies in ((after, own_next), (after & (place >= 1), pass_on)):

            @pl.when(there)
            def _():
                sent(copies(g))

        @pl.when(place >= 1)
        def _():
            backward(g, 0, 0, -1).wait_send()

        @pl.when(place >= 2)
        def _():
            backward(g, 1, 1, -2).wait_send()

    @pl.loop(0, KEY_VALUE_HEADS)
    def _(g):
        @pl.when((z == 0) | (z == hs_count - 2) | (straight(g) & after))
        def _():
            take(own_ref, 0, g)

        @pl.when(place + 2 < total)
        def _():
            take(own_ref, 1, g)

        dk_ref[:, cols(g)] = own_ref[:, cols(g)].astype(jnp.bfloat16)


def store_kernel(dq_ref, dk_ref, dq_hbm, dk_hbm, sem):
    copies = (
        pltpu.make_async_copy(dq_ref, dq_hbm, sem.at[0]),
        pltpu.make_async_copy(dk_ref, dk_hbm, sem.at[1]),
    )
    for copy in copies:
        copy.start()
    for copy in copies:
        copy.wait()


def shards(queries, key_matrix, value_matrix, output_gradient, doc_lengths, windows):
    rows = queries.shape[0]
    ctx_count, hs_count = lax.axis_size("ctx"), lax.axis_size("hs")
    if HALO * rows < WINDOW_LIMIT or hs_count < 3:
        raise ValueError("unsupported shape")
    groups = KEY_VALUE_HEADS
    ext = (HALO + 1) * rows
    kv_cols = key_matrix.shape[1]
    any_spec = pl.BlockSpec(memory_space=pltpu.HBM)
    grads = pl.pallas_call(
        functools.partial(attention_kernel, ctx_count, hs_count, rows),
        out_shape=(
            pltpu.VMEM(queries.shape, jnp.bfloat16),
            pltpu.VMEM(key_matrix.shape, jnp.bfloat16),
        ),
        in_specs=[any_spec, any_spec, any_spec, any_spec, any_spec, any_spec],
        out_specs=(pl.BlockSpec(memory_space=pltpu.VMEM), pl.BlockSpec(memory_space=pltpu.VMEM)),
        scratch_shapes=[
            pltpu.SMEM(doc_lengths.shape, jnp.int32),
            pltpu.SMEM(windows.shape, jnp.int32),
            pltpu.VMEM(queries.shape, jnp.bfloat16),
            pltpu.VMEM(queries.shape, jnp.bfloat16),
            pltpu.VMEM((ext, kv_cols), jnp.bfloat16),
            pltpu.VMEM((ext, kv_cols), jnp.bfloat16),
            pltpu.VMEM((rows, kv_cols), jnp.float32),
            pltpu.VMEM((ext, QUERY_HEADS // KEY_VALUE_HEADS * rows), jnp.bfloat16),
            pltpu.VMEM((QUERY_HEADS // KEY_VALUE_HEADS * rows, HEAD_SIZE), jnp.bfloat16),
            pltpu.VMEM((2, rows, kv_cols), jnp.bfloat16),
            pltpu.VMEM((3, rows, kv_cols), jnp.bfloat16),
            pltpu.SemaphoreType.DMA((2,)),
            pltpu.SemaphoreType.DMA((4, groups)),
            pltpu.SemaphoreType.DMA((2, 2, groups)),
            pltpu.SemaphoreType.DMA((2, HALO, groups)),
            pltpu.SemaphoreType.DMA((2, groups)),
            pltpu.SemaphoreType.DMA((3, groups)),
        ],
        compiler_params=pltpu.CompilerParams(collective_id=0, has_side_effects=True),
    )(doc_lengths, windows, queries, key_matrix, value_matrix, output_gradient)
    vmem_spec = pl.BlockSpec(memory_space=pltpu.VMEM)
    return pl.pallas_call(
        store_kernel,
        out_shape=(
            jax.ShapeDtypeStruct(queries.shape, jnp.bfloat16),
            jax.ShapeDtypeStruct(key_matrix.shape, jnp.bfloat16),
        ),
        in_specs=[pl.BlockSpec(memory_space=pl.ANY)] * 2,
        out_specs=(any_spec, any_spec),
        scratch_shapes=[pltpu.SemaphoreType.DMA((2,))],
        compiler_params=pltpu.CompilerParams(vmem_limit_bytes=2**20),
    )(*grads)


def solution(mesh):
    spec = P(("ctx", "hs"), None)
    return jax.shard_map(
        shards,
        mesh=mesh,
        in_specs=(spec, spec, spec, spec, P(), P()),
        out_specs=(spec, spec),
        check_vma=False,
    )
```
